32 devices in a mesh: chan: 8 (over y, x, core), beam: 4 (over z).
Axes of the slice: x: 2, y: 2, z: 4, core: 2. Of those that a mesh axis runs over, the one named last changes fastest.
Arguments:
- observed: bfloat16 [8, 12, 288, 3, 4096], P('beam', None, 'chan'), may hold values from -6 to 6
- beam_pattern: bfloat16 [8, 12, 4096], replicated, may hold values from 0.29882812 to 1
- correction: float32 [8, 288, 2, 3], P('beam', 'chan'), may hold values from -0.5 to 1.3
- block_tile: int32 [8, 12], replicated, may hold values from 0 to 3, as said below
- block_offset: int32 [8, 12], replicated, may hold values from 0 to 19
Outputs:
- faraday: bfloat16 [4, 20, 2, 512, 4096], P('beam', None, None, None, 'chan')
The draws below stay inside these ranges and needn't reach their ends.
Inputs may be any that keep to these rules, and one draw needn't show every extreme that they name: `block_tile`: group the beams as index j holds them (beams j * 2 to (j + 1) * 2 - 1) and the tiles likewise (tile o for group o). The blocks of the beams of one group lie on the tiles of one group at most 6 times, and exactly 6 times for some tile group, for every beam group.
All inputs are finite; a program needn't handle non-finite values.
Results may differ from the reference program's by a relative error of at most 0.0061.
Values may be sent and summed in bfloat16 or wider, within the bound.
No kernel may reach another device: no remote copies, remote signals or barrier semaphores. Data moves between devices by JAX's collectives and lax.ppermute only.
A program may use at most 128 MiB of HBM per device.

```python
import math
import jax
import jax.numpy as jnp
from jax import lax

CHANNELS = 288
DEPTHS = 512
BEAM_DEV = 2
BLK_BEAM = 12
PIX = 4096
TILE_DEV = 1
TILE_BLK = 20
CAP = 6
BEAMS = 8
TILES = 4


def routing_tables(key):
    base_key = jax.random.fold_in(key, 11)
    key_hot, key_busy, key_rows, key_local = jax.random.split(base_key, 4)
    owner_count = TILES // TILE_DEV
    row_count = BEAMS // BEAM_DEV
    block_count = BEAM_DEV * BLK_BEAM
    hottest = jax.random.randint(key_hot, (), 0, owner_count)
    busiest = (hottest + jax.random.randint(key_busy, (row_count,), 0, 2)) % owner_count

    def row_owners(row_key, chosen):
        key_others, key_order = jax.random.split(row_key)
        others = (chosen + 1 + jnp.arange((owner_count - 1) * CAP, dtype=jnp.int32) // CAP) % owner_count
        others = jax.random.permutation(key_others, others)
        listing = jnp.concatenate([jnp.full((CAP,), chosen, jnp.int32), others.astype(jnp.int32)])[:block_count]
        return jax.random.permutation(key_order, listing)
    owners_all = jax.vmap(row_owners)(jax.random.split(key_rows, row_count), busiest)
    local_slot = jax.random.randint(key_local, (row_count, block_count), 0, TILE_DEV * TILE_BLK)
    tile_ids = owners_all * TILE_DEV + local_slot // TILE_BLK
    offsets = local_slot % TILE_BLK
    return (tile_ids.reshape(BEAMS, BLK_BEAM).astype(jnp.int32), offsets.reshape(BEAMS, BLK_BEAM).astype(jnp.int32))


def draw_block_tile(key, part):
    return routing_tables(key)[0]


def draw_block_offset(key, part):
    return routing_tables(key)[1]


def draw_correction(key, part):
    key_diag, key_leak = jax.random.split(jax.random.fold_in(key, 5))
    leakage = jax.random.uniform(key_leak, (BEAMS, CHANNELS, 2, 3), jnp.float32, -0.35, 0.35)
    diagonal = jax.random.uniform(key_diag, (BEAMS, CHANNELS, 2, 1), jnp.float32, 0.7, 1.3)
    row_ids = jnp.arange(2, dtype=jnp.int32)[:, None]
    col_ids = jnp.arange(3, dtype=jnp.int32)[None, :]
    on_diag = (col_ids == row_ids + 1)[None, None, :, :]
    return jnp.where(on_diag, diagonal, leakage).astype(jnp.float32)


def block_scale(stream_key, dims, cuts, smallest, high):
    gain = 1.0
    for position, shards_of in cuts:
        draws = jax.random.uniform(jax.random.fold_in(jax.random.fold_in(stream_key, 6), position), (shards_of,), jnp.float32, smallest / len(cuts), high / len(cuts))
        gain = gain * jnp.repeat(jnp.exp(draws), dims[position] // shards_of).reshape((-1,) + (1,) * (len(dims) - 1 - position))
    return gain


def gaussian(stream_key, dims, scale, reach, cuts=(), held_as=jnp.bfloat16):
    result = scale * jax.random.normal(stream_key, dims, jnp.float32)
    if cuts:
        result = result * block_scale(stream_key, dims, cuts, -0.22, 0.18)
    return jnp.clip(result, -reach, reach).astype(held_as)


def setup_inputs(seed: int = 0) -> dict:
    keys = jax.random.split(jax.random.key(seed), 6)
    observed = gaussian(keys[0], (BEAMS, BLK_BEAM, CHANNELS, 3, PIX), 1.0, 6.0, ((0, 4), (2, 8)))
    beam_pattern = jnp.clip(jnp.exp(jax.random.uniform(keys[1], (BEAMS, BLK_BEAM, PIX), jnp.float32, math.log(0.29882812), math.log(1.0))), 0.29882812, 1.0).astype(jnp.bfloat16)
    correction = draw_correction(jax.random.fold_in(keys[5], 71), 0)
    block_tile = draw_block_tile(jax.random.fold_in(keys[5], 71), 0)
    block_offset = draw_block_offset(jax.random.fold_in(keys[5], 71), 0)
    return {"observed": observed, "beam_pattern": beam_pattern, "correction": correction, "block_tile": block_tile, "block_offset": block_offset}


floor_value = 0.25
band_mhz = 288.0
depth_step = 32.0

def faraday_table(channels, depths):
    chan_index = jnp.arange(channels, dtype=jnp.float32)
    frequency = 800.0 + (chan_index + 0.5) * (band_mhz / channels)
    lambda_sq = 299.792458 / frequency * (299.792458 / frequency)
    shifted = lambda_sq - jnp.mean(lambda_sq)
    depth_grid = (jnp.arange(depths, dtype=jnp.float32) - depths // 2) * depth_step
    phase_angle = 2.0 * depth_grid[:, None] * shifted[None, :]
    cosine = jnp.cos(phase_angle)
    sine_part = jnp.sin(phase_angle)
    real_rows = jnp.stack([cosine, sine_part], axis=2).reshape(depths, 2 * channels)
    imag_rows = jnp.stack([-sine_part, cosine], axis=2).reshape(depths, 2 * channels)
    table = jnp.concatenate([real_rows, imag_rows], axis=0) / jnp.sqrt(jnp.float32(channels))
    return table.astype(jnp.bfloat16)

def reference(observed, beam_pattern, correction, block_tile, block_offset):
    block_total = BEAMS * BLK_BEAM
    slot_of = (block_tile * TILE_BLK + block_offset).reshape(block_total).astype(jnp.int32)
    pattern_flat = beam_pattern.astype(jnp.float32).reshape(block_total, PIX)
    weight_all = jax.ops.segment_sum(pattern_flat * pattern_flat, slot_of, num_segments=TILES * TILE_BLK)
    flat_obs = observed.reshape(block_total, CHANNELS, 3, PIX)
    kernel = lax.optimization_barrier(faraday_table(CHANNELS, DEPTHS)).astype(jnp.float32)

    def one_tile(tile_index):

        def add_block(total_sum, block):
            beam_index = block // BLK_BEAM
            obs_block = lax.dynamic_index_in_dim(flat_obs, block, 0, keepdims=False)
            coefficient = lax.dynamic_index_in_dim(correction, beam_index, 0, keepdims=False)
            corrected = lax.optimization_barrier(jnp.sum(coefficient[:, :, :, None] * obs_block[:, None, :, :].astype(jnp.float32), axis=2))
            pattern_row = lax.dynamic_index_in_dim(pattern_flat, block, 0, keepdims=False)
            contrib = (pattern_row[None, None, :] * corrected).astype(jnp.bfloat16)
            contrib = lax.optimization_barrier(contrib).astype(jnp.float32)
            local_slot = lax.dynamic_index_in_dim(slot_of, block, 0, keepdims=False) - tile_index * TILE_BLK
            inside = (local_slot >= 0) & (local_slot < TILE_BLK)
            target = jnp.clip(local_slot, 0, TILE_BLK - 1).astype(jnp.int32)
            current = lax.dynamic_index_in_dim(total_sum, target, 0, keepdims=False)
            updated = current + jnp.where(inside, contrib, jnp.zeros_like(contrib))
            total_sum = lax.dynamic_update_index_in_dim(total_sum, updated, target, 0)
            return (total_sum, None)
        start_sum = jnp.zeros((TILE_BLK, CHANNELS, 2, PIX), jnp.float32)
        numerator, unused_out = lax.scan(add_block, start_sum, jnp.arange(block_total, dtype=jnp.int32))
        weight_sum = lax.dynamic_slice_in_dim(weight_all, (tile_index * TILE_BLK).astype(jnp.int32), TILE_BLK, 0)
        sky_image = (numerator / jnp.maximum(weight_sum, floor_value)[:, None, None, :]).astype(jnp.bfloat16)
        sky_image = lax.optimization_barrier(sky_image).astype(jnp.float32)
        spectrum = jnp.einsum('kx,lxp->lkp', kernel, sky_image.reshape(TILE_BLK, 2 * CHANNELS, PIX))
        return spectrum.astype(jnp.bfloat16).reshape(TILE_BLK, 2, DEPTHS, PIX)
    return lax.map(one_tile, jnp.arange(TILES, dtype=jnp.int32))
```

```python
import functools

import jax
import jax.numpy as jnp
from jax import lax
from jax.experimental import pallas as pl
from jax.experimental.pallas import tpu as pltpu
from jax.sharding import PartitionSpec as P

DEPTHS = 512
TILE_DEV = 1
TILE_BLK = 20
CAP = 6
LANES = 128


floor_value = 0.25
band_mhz = 288.0
depth_step = 32.0


def faraday_table(channels, depths):
    chan_index = jnp.arange(channels, dtype=jnp.float32)
    frequency = 800.0 + (chan_index + 0.5) * (band_mhz / channels)
    lambda_sq = 299.792458 / frequency * (299.792458 / frequency)
    shifted = lambda_sq - jnp.mean(lambda_sq)
    depth_grid = (jnp.arange(depths, dtype=jnp.float32) - depths // 2) * depth_step
    phase_angle = 2.0 * depth_grid[:, None] * shifted[None, :]
    cosine = jnp.cos(phase_angle)
    sine_part = jnp.sin(phase_angle)
    real_rows = jnp.stack([cosine, sine_part], axis=2).reshape(depths, 2 * channels)
    imag_rows = jnp.stack([-sine_part, cosine], axis=2).reshape(depths, 2 * channels)
    table = jnp.concatenate([real_rows, imag_rows], axis=0) / jnp.sqrt(jnp.float32(channels))
    return table.astype(jnp.bfloat16)


def routing(block_tile, beam_count, blocks_row):
    owner_of = (block_tile // TILE_DEV).reshape(beam_count, blocks_row)
    earlier = jnp.arange(blocks_row)[None, :] < jnp.arange(blocks_row)[:, None]
    same = owner_of[:, :, None] == owner_of[:, None, :]
    rank_in = jnp.sum((same & earlier[None]).astype(jnp.int32), axis=2)
    return (owner_of, rank_in)


def send_body(chan_count, blk_beam, owner_s, rank_s, *refs):
    obs_refs = refs[:chan_count]
    mix_ref, pattern_ref, out_ref = refs[chan_count:]
    rows = out_ref.shape[3]
    mix = mix_ref[0]
    for part in range(chan_count):
        pixels = obs_refs[part][0].reshape(-1, LANES)
        both = jnp.dot(mix, pixels, preferred_element_type=jnp.float32)
        corrected = both[:rows] + both[rows:]
        out_ref[0, part, 0] = (corrected * pattern_ref[0, part : part + 1]).astype(out_ref.dtype)


def send_chunk(obs_t, mix, pattern, owner, rank, chunk, beam_count, chan_count):
    blk_beam, chan_dev, stokes_in, beam_dev, pixels = obs_t.shape
    tiles = pixels // chan_count // LANES
    rows = chan_dev * 2
    obs_specs = [
        pl.BlockSpec(
            (1, chan_dev, stokes_in, beam_dev, LANES),
            lambda k, d, owner_s, rank_s, part=part: (k, 0, 0, 0, part * tiles + chunk),
        )
        for part in range(chan_count)
    ]
    return pl.pallas_call(
        functools.partial(send_body, chan_count, blk_beam),
        out_shape=jax.ShapeDtypeStruct((beam_count, chan_count, CAP, rows, LANES), jnp.bfloat16),
        grid_spec=pltpu.PrefetchScalarGridSpec(
            num_scalar_prefetch=2,
            grid=(blk_beam, beam_dev),
            in_specs=obs_specs
            + [
                pl.BlockSpec((1,) + mix.shape[1:], lambda k, d, owner_s, rank_s: (d, 0, 0)),
                pl.BlockSpec(
                    (1, chan_count, LANES), lambda k, d, owner_s, rank_s: (d * blk_beam + k, 0, 0)
                ),
            ],
            out_specs=pl.BlockSpec(
                (1, chan_count, 1, rows, LANES),
                lambda k, d, owner_s, rank_s: (
                    owner_s[d * blk_beam + k],
                    0,
                    rank_s[d * blk_beam + k],
                    0,
                    0,
                ),
            ),
        ),
        name=f"send_chunk_{chunk}",
    )(owner, rank, *([obs_t] * chan_count), mix, pattern)


def sky_body(pair, order_s, start_s, recv_ref, inverse_ref, table_ref, *refs):
    out_ref, total = refs[-2:]
    step = pl.program_id(0)
    parts, rows = recv_ref.shape[1], recv_ref.shape[3]
    total[...] = jnp.zeros_like(total)
    for side in range(pair):
        slot = step * pair + side

        def add(i, carry):
            source, rank = order_s[0, i], order_s[1, i]
            for part in range(parts):
                total[part * rows : (part + 1) * rows, side * LANES : (side + 1) * LANES] += recv_ref[
                    source, part, rank
                ].astype(jnp.float32)
            return carry

        lax.fori_loop(start_s[slot], start_s[slot + 1], add, 0)
    sky = jnp.concatenate(
        [
            total[:, side * LANES : (side + 1) * LANES] * inverse_ref[pl.ds(step * pair + side, 1)]
            for side in range(pair)
        ],
        axis=1,
    ).astype(jnp.bfloat16)
    spectrum = jnp.dot(table_ref[...], sky, preferred_element_type=jnp.float32)
    for side in range(pair):
        out_ref[side] = spectrum[:, side * LANES : (side + 1) * LANES].astype(out_ref.dtype)


def sky_chunk(recv, inverse, table, order, start, chunk, tiles, earlier):
    pair = 2
    slots = inverse.shape[0]
    whole = lambda a: pl.BlockSpec(a.shape, lambda l, *s: (0,) * a.ndim)
    in_specs = [whole(recv), whole(inverse), whole(table)]
    args = [order, start, recv, inverse, table]
    aliases = {}
    if earlier is not None:
        in_specs.append(pl.BlockSpec(memory_space=pl.ANY))
        aliases = {len(args): 0}
        args.append(earlier)
    return pl.pallas_call(
        functools.partial(sky_body, pair),
        out_shape=jax.ShapeDtypeStruct((slots, table.shape[0], tiles * LANES), jnp.bfloat16),
        grid_spec=pltpu.PrefetchScalarGridSpec(
            num_scalar_prefetch=2,
            grid=(slots // pair,),
            in_specs=in_specs,
            out_specs=pl.BlockSpec((pair, table.shape[0], LANES), lambda l, *s: (l, 0, chunk)),
            scratch_shapes=[pltpu.VMEM((table.shape[1], pair * LANES), jnp.float32)],
        ),
        input_output_aliases=aliases,
        compiler_params=pltpu.CompilerParams(vmem_limit_bytes=40 << 20),
        name=f"sky_chunk_{chunk}",
    )(*args)


def shards(observed, beam_pattern, correction, block_tile, block_offset):
    beam_count = lax.axis_size("beam")
    chan_count = lax.axis_size("chan")
    beam_row = lax.axis_index("beam")
    chan_part = lax.axis_index("chan")
    beam_dev, blk_beam, chan_dev, stokes_in, pixels = observed.shape
    pixel_share = pixels // chan_count
    tiles = pixel_share // LANES
    blocks_row = beam_dev * blk_beam
    local_slots = TILE_DEV * TILE_BLK
    rows = chan_dev * 2

    owner_of, rank_in = routing(block_tile, beam_count, blocks_row)
    my_owner = lax.dynamic_index_in_dim(owner_of, beam_row, 0, keepdims=False)
    my_rank = lax.dynamic_index_in_dim(rank_in, beam_row, 0, keepdims=False)

    same_chan = jnp.eye(chan_dev, dtype=jnp.float32)
    same_beam = jnp.eye(beam_dev, dtype=jnp.float32)
    mix = (
        correction[:, :, :, None, :, None]
        * same_chan[None, :, None, :, None, None]
        * same_beam[:, None, None, None, None, :]
    ).reshape(beam_dev, rows, chan_dev * stokes_in * beam_dev)
    mix_high = mix.astype(jnp.bfloat16)
    mix_low = (mix - mix_high.astype(jnp.float32)).astype(jnp.bfloat16)
    mix = jnp.concatenate([mix_high, mix_low], axis=1)

    own_pattern = lax.dynamic_slice_in_dim(beam_pattern, beam_row * beam_dev, beam_dev, 0)
    own_pattern = own_pattern.astype(jnp.float32).reshape(blocks_row, chan_count, tiles, LANES)
    obs_t = jnp.transpose(observed, (1, 2, 3, 0, 4))

    slot_of = (block_tile % TILE_DEV * TILE_BLK + block_offset).reshape(beam_count, blocks_row)
    mine = owner_of == beam_row
    ranks = jnp.arange(CAP, dtype=jnp.int32)
    hit = mine[:, :, None] & (rank_in[:, :, None] == ranks[None, None, :])
    entry_slot = jnp.min(jnp.where(hit, slot_of[:, :, None], local_slots), axis=1).reshape(-1)
    entries = beam_count * CAP
    index = jnp.arange(entries, dtype=jnp.int32)
    before = (entry_slot[None, :] < entry_slot[:, None]) | (
        (entry_slot[None, :] == entry_slot[:, None]) & (index[None, :] < index[:, None])
    )
    place = jnp.sum(before.astype(jnp.int32), axis=1)
    order = jnp.sum(jnp.where(place[None, :] == index[:, None], index[None, :], 0), axis=1)
    order = jnp.stack([order // CAP, order % CAP])
    slot_index = jnp.arange(local_slots + 1, dtype=jnp.int32)
    start = jnp.sum((entry_slot[None, :] < slot_index[:, None]).astype(jnp.int32), axis=1)

    global_slot = (block_tile * TILE_BLK + block_offset).reshape(-1)
    slot_range = beam_row * local_slots + jnp.arange(local_slots, dtype=jnp.int32)
    cover = (global_slot[None, :] == slot_range[:, None]).astype(jnp.float32)
    share = lax.dynamic_slice_in_dim(beam_pattern, chan_part * pixel_share, pixel_share, 2)
    share = share.astype(jnp.float32).reshape(-1, pixel_share)
    weight_sum = jnp.dot(cover, share * share, precision=lax.Precision.HIGHEST)
    inverse = 1.0 / jnp.maximum(weight_sum, floor_value)
    table = faraday_table(chan_dev * chan_count, DEPTHS)

    spectrum = None
    for chunk in range(tiles):
        sent = send_chunk(
            obs_t, mix, own_pattern[:, :, chunk], my_owner, my_rank, chunk, beam_count, chan_count
        )
        received = lax.all_to_all(
            sent.reshape((beam_count * chan_count,) + sent.shape[2:]),
            ("beam", "chan"),
            split_axis=0,
            concat_axis=0,
            tiled=True,
        ).reshape(sent.shape)
        spectrum = sky_chunk(
            received,
            inverse[:, chunk * LANES : (chunk + 1) * LANES],
            table,
            order,
            start,
            chunk,
            tiles,
            spectrum,
        )
    return spectrum.reshape(TILE_DEV, TILE_BLK, 2, DEPTHS, pixel_share)


def solution(mesh):
    placed = (P("beam", None, "chan", None, None), P(), P("beam", "chan", None, None), P(), P())
    return jax.shard_map(
        shards,
        mesh=mesh,
        in_specs=placed,
        out_specs=P("beam", None, None, None, "chan"),
        check_vma=False,
    )
```

```python
import functools

import jax
import jax.numpy as jnp
from jax import lax
from jax.experimental import pallas as pl
from jax.experimental.pallas import tpu as pltpu
from jax.sharding import PartitionSpec as P

DEPTHS = 512
TILE_DEV = 1
TILE_BLK = 20
CAP = 6
LANES = 128


floor_value = 0.25
band_mhz = 288.0
depth_step = 32.0


def faraday_table(parts, part_channels, depths):
    channels = parts * part_channels
    chan_index = jnp.arange(channels, dtype=jnp.float32)
    frequency = 800.0 + (chan_index + 0.5) * (band_mhz / channels)
    lambda_sq = 299.792458 / frequency * (299.792458 / frequency)
    shifted = lambda_sq - jnp.mean(lambda_sq)
    depth_grid = (jnp.arange(depths, dtype=jnp.float32) - depths // 2) * depth_step
    phase_angle = 2.0 * depth_grid[:, None] * shifted[None, :]
    cosine = jnp.cos(phase_angle).reshape(depths, parts, part_channels)
    sine_part = jnp.sin(phase_angle).reshape(depths, parts, part_channels)
    real_rows = jnp.stack([cosine, sine_part], axis=2).reshape(depths, 2 * channels)
    imag_rows = jnp.stack([-sine_part, cosine], axis=2).reshape(depths, 2 * channels)
    table = jnp.concatenate([real_rows, imag_rows], axis=0) / jnp.sqrt(jnp.float32(channels))
    return table.astype(jnp.bfloat16)


def send_body(
    first_tile,
    width,
    obs,
    pattern,
    tile_s,
    corr_ref,
    out,
    mix,
    obs_buf,
    pat_buf,
    pat_wide,
    out_buf,
    count,
    in_sem,
    pat_sem,
    out_sem,
):
    blk_beam, chan_dev, stokes_in, beam_dev, pixels = obs.shape
    beam_count, chan_count = out.shape[:2]
    beams = pattern.shape[1]
    tiles = pixels // chan_count // LANES
    depth = obs_buf.shape[0]
    lanes = width * LANES
    rows = 2 * chan_dev
    beam_row = lax.axis_index("beam")

    def obs_copies(k, slot):
        return [
            pltpu.make_async_copy(
                obs.at[k, :, :, :, pl.ds((part * tiles + first_tile + w) * LANES, LANES)],
                obs_buf.at[slot, part * width + w],
                in_sem.at[slot, part * width + w],
            )
            for part in range(chan_count)
            for w in range(width)
        ]

    def out_copy(slot, d, owner, rank):
        return pltpu.make_async_copy(
            out_buf.at[slot, d], out.at[owner, :, rank], out_sem.at[slot, d]
        )

    pat_copies = [
        pltpu.make_async_copy(
            pattern.at[:, :, pl.ds((part * tiles + first_tile) * LANES, lanes)],
            pat_buf.at[part],
            pat_sem.at[part],
        )
        for part in range(chan_count)
    ]
    for copy in obs_copies(0, 0) + pat_copies:
        copy.start()
    for k in range(1, depth):
        for copy in obs_copies(k, k):
            copy.start()

    identity = (
        lax.broadcasted_iota(jnp.int32, (chan_dev, chan_dev), 0)
        == lax.broadcasted_iota(jnp.int32, (chan_dev, chan_dev), 1)
    ).astype(jnp.float32)
    columns = lax.dot_general(
        identity,
        corr_ref[...],
        (((1,), (1,)), ((), ())),
        precision=lax.Precision.HIGHEST,
        preferred_element_type=jnp.float32,
    )
    inner = stokes_in * beam_dev
    wide = (chan_dev, chan_dev * inner)
    offset = lax.broadcasted_iota(jnp.int32, wide, 1) - inner * lax.broadcasted_iota(jnp.int32, wide, 0)
    high, low = [], []
    for d in range(beam_dev):
        for s in range(2):
            block = jnp.zeros(wide, jnp.float32)
            for t in range(stokes_in):
                column = (d * stokes_in + t) * 2 + s
                block = jnp.where(offset == t * beam_dev + d, columns[:, column : column + 1], block)
            top = block.astype(jnp.bfloat16).astype(jnp.float32)
            high.append(top)
            low.append(block - top)
    mix[...] = jnp.concatenate(high + low, axis=0).astype(jnp.bfloat16)

    for owner in range(beam_count):
        count[owner] = 0
    for copy in pat_copies:
        copy.wait()
    for part in range(chan_count):
        for w in range(width):
            for k in range(blk_beam):
                pat_wide[part * width + w, k * beams : (k + 1) * beams] = pat_buf[
                    part, k, :, w * LANES : (w + 1) * LANES
                ].astype(jnp.float32)

    def block(k, carry):
        slot = lax.rem(k, depth)
        side = lax.rem(k, 2)
        for copy in obs_copies(k, slot):
            copy.wait()

        @pl.when(k >= 2)
        def _():
            for d in range(beam_dev):
                out_copy(side, d, 0, 0).wait()

        for part in range(chan_count):
            for w in range(width):
                observed = obs_buf[slot, part * width + w].reshape(-1, LANES)
                mixed = jnp.dot(mix[...], observed, preferred_element_type=jnp.float32)
                corrected = mixed[: beam_dev * rows] + mixed[beam_dev * rows :]
                for d in range(beam_dev):
                    weight = pat_wide[
                        part * width + w, pl.ds(k * beams + beam_row * beam_dev + d, 1)
                    ]
                    out_buf[side, d, part, :, w * LANES : (w + 1) * LANES] = (
                        corrected[d * rows : (d + 1) * rows] * weight
                    ).astype(jnp.bfloat16)
        for d in range(beam_dev):
            owner = tile_s[beam_row * beam_dev + d, k] // TILE_DEV
            rank = count[owner]
            count[owner] = rank + 1
            out_copy(side, d, owner, rank).start()

        @pl.when(k + depth < blk_beam)
        def _():
            for copy in obs_copies(k + depth, slot):
                copy.start()

        return carry

    lax.fori_loop(0, blk_beam, block, 0)
    for side in range(2):
        for d in range(beam_dev):
            out_copy(side, d, 0, 0).wait()


def send_chunk(obs_t, pattern_t, block_tile, corr_t, beam_count, chan_count, first_tile, width):
    blk_beam, chan_dev, stokes_in, beam_dev, pixels = obs_t.shape
    rows = chan_dev * 2
    lanes = width * LANES
    beams = pattern_t.shape[1]
    depth = 4
    anywhere = pl.BlockSpec(memory_space=pltpu.HBM)
    return pl.pallas_call(
        functools.partial(send_body, first_tile, width),
        out_shape=jax.ShapeDtypeStruct((beam_count, chan_count, CAP, rows, lanes), jnp.bfloat16),
        in_specs=[
            anywhere,
            anywhere,
            pl.BlockSpec(memory_space=pltpu.SMEM),
            pl.BlockSpec(memory_space=pltpu.VMEM),
        ],
        out_specs=anywhere,
        scratch_shapes=[
            pltpu.VMEM((2 * beam_dev * rows, chan_dev * stokes_in * beam_dev), jnp.bfloat16),
            pltpu.VMEM(
                (depth, chan_count * width, chan_dev, stokes_in, beam_dev, LANES), jnp.bfloat16
            ),
            pltpu.VMEM((chan_count, blk_beam, beams, lanes), jnp.bfloat16),
            pltpu.VMEM((chan_count * width, blk_beam * beams, LANES), jnp.float32),
            pltpu.VMEM((2, beam_dev, chan_count, rows, lanes), jnp.bfloat16),
            pltpu.SMEM((beam_count,), jnp.int32),
            pltpu.SemaphoreType.DMA((depth, chan_count * width)),
            pltpu.SemaphoreType.DMA((chan_count,)),
            pltpu.SemaphoreType.DMA((2, beam_dev)),
        ],
        compiler_params=pltpu.CompilerParams(vmem_limit_bytes=48 << 20),
        name=f"send_tile_{first_tile}",
    )(obs_t, pattern_t, block_tile, corr_t)


def sky_body(pair, first_tile, order_s, start_s, recv, inverse_ref, table_ref, *refs):
    out_ref, blocks, total, sem = refs[-4:]
    step = pl.program_id(0)
    parts, rows, lanes = blocks.shape[1:]
    entries = blocks.shape[0]
    slots = pair * pl.num_programs(0)

    def entry_copy(i, source, rank):
        return pltpu.make_async_copy(recv.at[source, :, rank], blocks.at[i], sem.at[i])

    @pl.when(step == 0)
    def _():
        def begin(i, carry):
            entry_copy(i, order_s[0, i], order_s[1, i]).start()
            return carry

        lax.fori_loop(0, start_s[slots], begin, 0)

    for side in range(pair):
        slot = step * pair + side
        columns = slice(side * lanes, (side + 1) * lanes)
        total[:, columns] = jnp.zeros_like(total[:, columns])

        def add(i, carry):
            entry_copy(i, 0, 0).wait()
            for part in range(parts):
                total[part * rows : (part + 1) * rows, columns] += blocks[i, part].astype(jnp.float32)
            return carry

        lax.fori_loop(start_s[slot], start_s[slot + 1], add, 0)
    tiles = lanes // LANES
    sky = jnp.concatenate(
        [
            total[:, tile * LANES : (tile + 1) * LANES]
            * inverse_ref[first_tile + tile % tiles, pl.ds(step * pair + tile // tiles, 1)]
            for tile in range(pair * tiles)
        ],
        axis=1,
    ).astype(jnp.bfloat16)
    spectrum = jnp.dot(table_ref[...], sky, preferred_element_type=jnp.float32)
    for side in range(pair):
        out_ref[side] = spectrum[:, side * lanes : (side + 1) * lanes].astype(out_ref.dtype)


def sky_chunk(recv, inverse, table, order, start, first_tile, width, tiles, earlier):
    pair = 2
    slots = inverse.shape[1]
    lanes = width * LANES
    beam_count, parts, capacity, rows = recv.shape[:4]
    anywhere = pl.BlockSpec(memory_space=pltpu.HBM)
    whole = lambda a: pl.BlockSpec(a.shape, lambda l, *s: (0,) * a.ndim)
    in_specs = [anywhere, whole(inverse), whole(table)]
    args = [order, start, recv, inverse, table]
    aliases = {}
    if earlier is not None:
        in_specs.append(anywhere)
        aliases = {len(args): 0}
        args.append(earlier)
    return pl.pallas_call(
        functools.partial(sky_body, pair, first_tile),
        out_shape=jax.ShapeDtypeStruct((slots, table.shape[0], tiles * LANES), jnp.bfloat16),
        grid_spec=pltpu.PrefetchScalarGridSpec(
            num_scalar_prefetch=2,
            grid=(slots // pair,),
            in_specs=in_specs,
            out_specs=pl.BlockSpec(
                (pl.Element(pair), pl.Element(table.shape[0]), pl.Element(lanes)),
                lambda l, *s: (l * pair, 0, first_tile * LANES),
            ),
            scratch_shapes=[
                pltpu.VMEM((beam_count * capacity, parts, rows, lanes), jnp.bfloat16),
                pltpu.VMEM((table.shape[1], pair * lanes), jnp.float32),
                pltpu.SemaphoreType.DMA((beam_count * capacity,)),
            ],
        ),
        input_output_aliases=aliases,
        compiler_params=pltpu.CompilerParams(vmem_limit_bytes=48 << 20),
        name=f"sky_tile_{first_tile}",
    )(*args)


def received_order(block_tile, block_offset, beam_row, beam_count, beam_dev, blk_beam):
    local_slots = TILE_DEV * TILE_BLK

    def by_block(a):
        return jnp.swapaxes(a.reshape(beam_count, beam_dev, blk_beam), 1, 2).reshape(beam_count, -1)

    tile = by_block(block_tile)
    slot_of = tile % TILE_DEV * TILE_BLK + by_block(block_offset)
    mine = tile // TILE_DEV == beam_row
    position = jnp.arange(beam_dev * blk_beam, dtype=jnp.int32)
    earlier = position[None, :] < position[:, None]
    rank_in = jnp.sum((mine[:, None, :] & earlier[None]).astype(jnp.int32), axis=2)
    ranks = jnp.arange(CAP, dtype=jnp.int32)
    hit = mine[:, :, None] & (rank_in[:, :, None] == ranks[None, None, :])
    entry_slot = jnp.min(jnp.where(hit, slot_of[:, :, None], local_slots), axis=1).reshape(-1)
    index = jnp.arange(beam_count * CAP, dtype=jnp.int32)
    before = (entry_slot[None, :] < entry_slot[:, None]) | (
        (entry_slot[None, :] == entry_slot[:, None]) & (index[None, :] < index[:, None])
    )
    place = jnp.sum(before.astype(jnp.int32), axis=1)
    order = jnp.sum(jnp.where(place[None, :] == index[:, None], index[None, :], 0), axis=1)
    slot_index = jnp.arange(local_slots + 1, dtype=jnp.int32)
    start = jnp.sum((entry_slot[None, :] < slot_index[:, None]).astype(jnp.int32), axis=1)
    return jnp.stack([order // CAP, order % CAP]), start


def pixel_chunks(tiles):
    if tiles < 4:
        return [(tile, 1) for tile in range(tiles)]
    return [(0, 1), (1, tiles - 2), (tiles - 1, 1)]


def shards(observed, beam_pattern, correction, block_tile, block_offset):
    beam_count = lax.axis_size("beam")
    chan_count = lax.axis_size("chan")
    beam_row = lax.axis_index("beam")
    chan_part = lax.axis_index("chan")
    beam_dev, blk_beam, chan_dev, stokes_in, pixels = observed.shape
    pixel_share = pixels // chan_count
    tiles = pixel_share // LANES
    local_slots = TILE_DEV * TILE_BLK

    obs_t = jnp.transpose(observed, (1, 2, 3, 0, 4))
    pattern_t = jnp.transpose(beam_pattern, (1, 0, 2))
    corr_t = jnp.transpose(correction, (0, 3, 2, 1)).reshape(-1, chan_dev)

    order, start = received_order(
        block_tile, block_offset, beam_row, beam_count, beam_dev, blk_beam
    )
    global_slot = (block_tile * TILE_BLK + block_offset).reshape(-1)
    slot_range = beam_row * local_slots + jnp.arange(local_slots, dtype=jnp.int32)
    cover = (global_slot[None, :] == slot_range[:, None]).astype(jnp.float32)
    share = lax.dynamic_slice_in_dim(beam_pattern, chan_part * pixel_share, pixel_share, 2)
    share = share.astype(jnp.float32).reshape(-1, pixel_share)
    weight_sum = jnp.dot(cover, share * share, precision=lax.Precision.HIGHEST)
    inverse = 1.0 / jnp.maximum(weight_sum, floor_value)
    inverse = jnp.swapaxes(inverse.reshape(local_slots, tiles, LANES), 0, 1)
    table = faraday_table(chan_count, chan_dev, DEPTHS)

    spectrum = None
    for first_tile, width in pixel_chunks(tiles):
        sent = send_chunk(
            obs_t, pattern_t, block_tile, corr_t, beam_count, chan_count, first_tile, width
        )
        received = lax.all_to_all(
            sent.reshape((beam_count * chan_count,) + sent.shape[2:]),
            ("beam", "chan"),
            split_axis=0,
            concat_axis=0,
            tiled=True,
        ).reshape(sent.shape)
        spectrum = sky_chunk(
            received,
            inverse,
            table,
            order,
            start,
            first_tile,
            width,
            tiles,
            spectrum,
        )
    return spectrum.reshape(TILE_DEV, TILE_BLK, 2, DEPTHS, pixel_share)


def solution(mesh):
    placed = (P("beam", None, "chan", None, None), P(), P("beam", "chan", None, None), P(), P())
    return jax.shard_map(
        shards,
        mesh=mesh,
        in_specs=placed,
        out_specs=P("beam", None, None, None, "chan"),
        check_vma=False,
    )
```

```python
import functools

import jax
import jax.numpy as jnp
from jax import lax
from jax.experimental import pallas as pl
from jax.experimental.pallas import tpu as pltpu
from jax.sharding import PartitionSpec as P

DEPTHS = 512
TILE_DEV = 1
TILE_BLK = 20
CAP = 6
LANES = 128


floor_value = 0.25
band_mhz = 288.0
depth_step = 32.0


def faraday_table(parts, part_channels, depths):
    channels = parts * part_channels
    chan_index = jnp.arange(channels, dtype=jnp.float32)
    frequency = 800.0 + (chan_index + 0.5) * (band_mhz / channels)
    lambda_sq = 299.792458 / frequency * (299.792458 / frequency)
    shifted = lambda_sq - jnp.mean(lambda_sq)
    depth_grid = (jnp.arange(depths, dtype=jnp.float32) - depths // 2) * depth_step
    phase_angle = 2.0 * depth_grid[:, None] * shifted[None, :]
    cosine = jnp.cos(phase_angle).reshape(depths, parts, part_channels)
    sine_part = jnp.sin(phase_angle).reshape(depths, parts, part_channels)
    real_rows = jnp.stack([cosine, sine_part], axis=2).reshape(depths, 2 * channels)
    imag_rows = jnp.stack([-sine_part, cosine], axis=2).reshape(depths, 2 * channels)
    table = jnp.concatenate([real_rows, imag_rows], axis=0) / jnp.sqrt(jnp.float32(channels))
    return table.astype(jnp.bfloat16)


def in_hbm(array):
    return pltpu.with_memory_space_constraint(array, pltpu.HBM)


def send_body(
    first_tile,
    width,
    obs,
    pattern,
    block_tile,
    correction,
    out,
    tile_s,
    corr_ref,
    mix,
    obs_buf,
    pat_buf,
    pat_wide,
    out_buf,
    count,
    in_sem,
    pat_sem,
    out_sem,
    tile_sem,
    corr_sem,
):
    blk_beam, chan_dev, stokes_in, beam_dev, pixels = obs.shape
    beam_count, chan_count = out.shape[:2]
    beams = pattern.shape[1]
    tiles = pixels // chan_count // LANES
    depth = obs_buf.shape[0]
    lanes = width * LANES
    rows = 2 * chan_dev
    beam_row = lax.axis_index("beam")

    def obs_copies(k, slot):
        return [
            pltpu.make_async_copy(
                obs.at[k, :, :, :, pl.ds((part * tiles + first_tile + w) * LANES, LANES)],
                obs_buf.at[slot, part * width + w],
                in_sem.at[slot, part * width + w],
            )
            for part in range(chan_count)
            for w in range(width)
        ]

    def out_copy(slot, d, owner, rank):
        return pltpu.make_async_copy(
            out_buf.at[slot, d], out.at[owner, :, rank], out_sem.at[slot, d]
        )

    pat_copies = [
        pltpu.make_async_copy(
            pattern.at[:, :, pl.ds((part * tiles + first_tile) * LANES, lanes)],
            pat_buf.at[part],
            pat_sem.at[part],
        )
        for part in range(chan_count)
    ]
    tile_copy = pltpu.make_async_copy(block_tile, tile_s, tile_sem)
    corr_copy = pltpu.make_async_copy(correction, corr_ref, corr_sem)
    corr_copy.start()
    for copy in obs_copies(0, 0) + pat_copies + [tile_copy]:
        copy.start()
    for k in range(1, depth):
        for copy in obs_copies(k, k):
            copy.start()

    identity = (
        lax.broadcasted_iota(jnp.int32, (chan_dev, chan_dev), 0)
        == lax.broadcasted_iota(jnp.int32, (chan_dev, chan_dev), 1)
    ).astype(jnp.float32)
    corr_copy.wait()
    columns = [
        [
            lax.dot_general(
                identity,
                corr_ref[d, t],
                (((1,), (1,)), ((), ())),
                precision=lax.Precision.HIGHEST,
                preferred_element_type=jnp.float32,
            )
            for t in range(stokes_in)
        ]
        for d in range(beam_dev)
    ]
    inner = stokes_in * beam_dev
    wide = (chan_dev, chan_dev * inner)
    offset = lax.broadcasted_iota(jnp.int32, wide, 1) - inner * lax.broadcasted_iota(jnp.int32, wide, 0)
    high, low = [], []
    for d in range(beam_dev):
        for s in range(2):
            block = jnp.zeros(wide, jnp.float32)
            for t in range(stokes_in):
                block = jnp.where(offset == t * beam_dev + d, columns[d][t][:, s : s + 1], block)
            top = block.astype(jnp.bfloat16).astype(jnp.float32)
            high.append(top)
            low.append(block - top)
    mix[...] = jnp.concatenate(high + low, axis=0).astype(jnp.bfloat16)

    for owner in range(beam_count):
        count[owner] = 0
    for copy in pat_copies + [tile_copy]:
        copy.wait()
    for part in range(chan_count):
        for w in range(width):
            for k in range(blk_beam):
                pat_wide[part * width + w, k * beams : (k + 1) * beams] = pat_buf[
                    part, k, :, w * LANES : (w + 1) * LANES
                ].astype(jnp.float32)

    def block(k, carry):
        slot = lax.rem(k, depth)
        side = lax.rem(k, 2)
        for copy in obs_copies(k, slot):
            copy.wait()

        @pl.when(k >= 2)
        def _():
            for d in range(beam_dev):
                out_copy(side, d, 0, 0).wait()

        for part in range(chan_count):
            for w in range(width):
                observed = obs_buf[slot, part * width + w].reshape(-1, LANES)
                mixed = jnp.dot(mix[...], observed, preferred_element_type=jnp.float32)
                corrected = mixed[: beam_dev * rows] + mixed[beam_dev * rows :]
                for d in range(beam_dev):
                    weight = pat_wide[
                        part * width + w, pl.ds(k * beams + beam_row * beam_dev + d, 1)
                    ]
                    out_buf[side, d, part, :, w * LANES : (w + 1) * LANES] = (
                        corrected[d * rows : (d + 1) * rows] * weight
                    ).astype(jnp.bfloat16)
        for d in range(beam_dev):
            owner = tile_s[beam_row * beam_dev + d, k] // TILE_DEV
            rank = count[owner]
            count[owner] = rank + 1
            out_copy(side, d, owner, rank).start()

        @pl.when(k + depth < blk_beam)
        def _():
            for copy in obs_copies(k + depth, slot):
                copy.start()

        return carry

    lax.fori_loop(0, blk_beam, block, 0)
    for side in range(2):
        for d in range(beam_dev):
            out_copy(side, d, 0, 0).wait()


def send_chunk(obs_t, pattern_t, block_tile, corr_t, beam_count, chan_count, first_tile, width):
    blk_beam, chan_dev, stokes_in, beam_dev, pixels = obs_t.shape
    rows = chan_dev * 2
    lanes = width * LANES
    beams = pattern_t.shape[1]
    depth = 4
    anywhere = pl.BlockSpec(memory_space=pltpu.HBM)
    return pl.pallas_call(
        functools.partial(send_body, first_tile, width),
        out_shape=pltpu.HBM((beam_count, chan_count, CAP, rows, lanes), jnp.bfloat16),
        in_specs=[
            anywhere,
            anywhere,
            anywhere,
            anywhere,
        ],
        out_specs=anywhere,
        scratch_shapes=[
            pltpu.SMEM(block_tile.shape, jnp.int32),
            pltpu.VMEM(corr_t.shape, jnp.float32),
            pltpu.VMEM((2 * beam_dev * rows, chan_dev * stokes_in * beam_dev), jnp.bfloat16),
            pltpu.VMEM(
                (depth, chan_count * width, chan_dev, stokes_in, beam_dev, LANES), jnp.bfloat16
            ),
            pltpu.VMEM((chan_count, blk_beam, beams, lanes), jnp.bfloat16),
            pltpu.VMEM((chan_count * width, blk_beam * beams, LANES), jnp.float32),
            pltpu.VMEM((2, beam_dev, chan_count, rows, lanes), jnp.bfloat16),
            pltpu.SMEM((beam_count,), jnp.int32),
            pltpu.SemaphoreType.DMA((depth, chan_count * width)),
            pltpu.SemaphoreType.DMA((chan_count,)),
            pltpu.SemaphoreType.DMA((2, beam_dev)),
            pltpu.SemaphoreType.DMA(()),
            pltpu.SemaphoreType.DMA(()),
        ],
        compiler_params=pltpu.CompilerParams(vmem_limit_bytes=61 << 20),
        name=f"send_tile_{first_tile}",
    )(obs_t, in_hbm(pattern_t), in_hbm(block_tile), in_hbm(corr_t))


def sky_body(pair, first_tile, order_s, start_s, recv, inverse_ref, table_ref, *refs):
    out_ref, blocks, total, sem = refs[-4:]
    step = pl.program_id(0)
    parts, rows, lanes = blocks.shape[1:]
    entries = blocks.shape[0]
    slots = pair * pl.num_programs(0)

    def entry_copy(i, source, rank):
        return pltpu.make_async_copy(recv.at[source, :, rank], blocks.at[i], sem.at[i])

    @pl.when(step == 0)
    def _():
        def begin(i, carry):
            entry_copy(i, order_s[0, i], order_s[1, i]).start()
            return carry

        lax.fori_loop(0, start_s[slots], begin, 0)

    for side in range(pair):
        slot = step * pair + side
        columns = slice(side * lanes, (side + 1) * lanes)
        total[:, columns] = jnp.zeros_like(total[:, columns])

        def add(i, carry):
            entry_copy(i, 0, 0).wait()
            for part in range(parts):
                total[part * rows : (part + 1) * rows, columns] += blocks[i, part].astype(jnp.float32)
            return carry

        lax.fori_loop(start_s[slot], start_s[slot + 1], add, 0)
    tiles = lanes // LANES
    sky = jnp.concatenate(
        [
            total[:, tile * LANES : (tile + 1) * LANES]
            * inverse_ref[first_tile + tile % tiles, pl.ds(step * pair + tile // tiles, 1)]
            for tile in range(pair * tiles)
        ],
        axis=1,
    ).astype(jnp.bfloat16)
    spectrum = jnp.dot(table_ref[...], sky, preferred_element_type=jnp.float32)
    for side in range(pair):
        out_ref[side] = spectrum[:, side * lanes : (side + 1) * lanes].astype(out_ref.dtype)


def sky_chunk(recv, inverse, table, order, start, first_tile, width, tiles, earlier):
    pair = 4
    slots = inverse.shape[1]
    lanes = width * LANES
    beam_count, parts, capacity, rows = recv.shape[:4]
    anywhere = pl.BlockSpec(memory_space=pltpu.HBM)
    whole = lambda a: pl.BlockSpec(a.shape, lambda l, *s: (0,) * a.ndim)
    in_specs = [anywhere, whole(inverse), whole(table)]
    args = [order, start, in_hbm(recv), inverse, table]
    aliases = {}
    if earlier is not None:
        in_specs.append(anywhere)
        aliases = {len(args): 0}
        args.append(earlier)
    return pl.pallas_call(
        functools.partial(sky_body, pair, first_tile),
        out_shape=jax.ShapeDtypeStruct((slots, table.shape[0], tiles * LANES), jnp.bfloat16),
        grid_spec=pltpu.PrefetchScalarGridSpec(
            num_scalar_prefetch=2,
            grid=(slots // pair,),
            in_specs=in_specs,
            out_specs=pl.BlockSpec(
                (pl.Element(pair), pl.Element(table.shape[0]), pl.Element(lanes)),
                lambda l, *s: (l * pair, 0, first_tile * LANES),
            ),
            scratch_shapes=[
                pltpu.VMEM((beam_count * capacity, parts, rows, lanes), jnp.bfloat16),
                pltpu.VMEM((table.shape[1], pair * lanes), jnp.float32),
                pltpu.SemaphoreType.DMA((beam_count * capacity,)),
            ],
        ),
        input_output_aliases=aliases,
        compiler_params=pltpu.CompilerParams(vmem_limit_bytes=48 << 20),
        name=f"sky_tile_{first_tile}",
    )(*args)


def received_order(block_tile, block_offset, beam_row, beam_count, beam_dev, blk_beam):
    local_slots = TILE_DEV * TILE_BLK

    def by_block(a):
        return jnp.swapaxes(a.reshape(beam_count, beam_dev, blk_beam), 1, 2).reshape(beam_count, -1)

    tile = by_block(block_tile)
    slot_of = tile % TILE_DEV * TILE_BLK + by_block(block_offset)
    mine = tile // TILE_DEV == beam_row
    position = jnp.arange(beam_dev * blk_beam, dtype=jnp.int32)
    earlier = position[None, :] < position[:, None]
    rank_in = jnp.sum((mine[:, None, :] & earlier[None]).astype(jnp.int32), axis=2)
    ranks = jnp.arange(CAP, dtype=jnp.int32)
    hit = mine[:, :, None] & (rank_in[:, :, None] == ranks[None, None, :])
    entry_slot = jnp.min(jnp.where(hit, slot_of[:, :, None], local_slots), axis=1).reshape(-1)
    index = jnp.arange(beam_count * CAP, dtype=jnp.int32)
    before = (entry_slot[None, :] < entry_slot[:, None]) | (
        (entry_slot[None, :] == entry_slot[:, None]) & (index[None, :] < index[:, None])
    )
    place = jnp.sum(before.astype(jnp.int32), axis=1)
    order = jnp.sum(jnp.where(place[None, :] == index[:, None], index[None, :], 0), axis=1)
    slot_index = jnp.arange(local_slots + 1, dtype=jnp.int32)
    start = jnp.sum((entry_slot[None, :] < slot_index[:, None]).astype(jnp.int32), axis=1)
    return jnp.stack([order // CAP, order % CAP]), start


def pixel_chunks(tiles):
    if tiles < 4:
        return [(tile, 1) for tile in range(tiles)]
    return [(0, 1), (1, tiles - 2), (tiles - 1, 1)]


def shards(observed, beam_pattern, correction, block_tile, block_offset):
    beam_count = lax.axis_size("beam")
    chan_count = lax.axis_size("chan")
    beam_row = lax.axis_index("beam")
    chan_part = lax.axis_index("chan")
    beam_dev, blk_beam, chan_dev, stokes_in, pixels = observed.shape
    pixel_share = pixels // chan_count
    tiles = pixel_share // LANES
    local_slots = TILE_DEV * TILE_BLK

    obs_t = jnp.transpose(observed, (1, 2, 3, 0, 4))
    pattern_t = jnp.transpose(beam_pattern, (1, 0, 2))
    corr_t = jnp.transpose(correction, (0, 3, 2, 1))

    order, start = received_order(
        block_tile, block_offset, beam_row, beam_count, beam_dev, blk_beam
    )
    global_slot = (block_tile * TILE_BLK + block_offset).reshape(-1)
    slot_range = beam_row * local_slots + jnp.arange(local_slots, dtype=jnp.int32)
    cover = (global_slot[None, :] == slot_range[:, None]).astype(jnp.float32)
    share = lax.dynamic_slice_in_dim(beam_pattern, chan_part * pixel_share, pixel_share, 2)
    share = share.astype(jnp.float32).reshape(-1, pixel_share)
    weight_sum = jnp.dot(cover, share * share, precision=lax.Precision.HIGHEST)
    inverse = 1.0 / jnp.maximum(weight_sum, floor_value)
    inverse = jnp.swapaxes(inverse.reshape(local_slots, tiles, LANES), 0, 1)
    table = faraday_table(chan_count, chan_dev, DEPTHS)

    spectrum = None
    for first_tile, width in pixel_chunks(tiles):
        sent = send_chunk(
            obs_t, pattern_t, block_tile, corr_t, beam_count, chan_count, first_tile, width
        )
        received = lax.all_to_all(
            sent.reshape((beam_count * chan_count,) + sent.shape[2:]),
            ("beam", "chan"),
            split_axis=0,
            concat_axis=0,
            tiled=True,
        ).reshape(sent.shape)
        spectrum = sky_chunk(
            received,
            inverse,
            table,
            order,
            start,
            first_tile,
            width,
            tiles,
            spectrum,
        )
    return spectrum.reshape(TILE_DEV, TILE_BLK, 2, DEPTHS, pixel_share)


def solution(mesh):
    placed = (P("beam", None, "chan", None, None), P(), P("beam", "chan", None, None), P(), P())
    return jax.shard_map(
        shards,
        mesh=mesh,
        in_specs=placed,
        out_specs=P("beam", None, None, None, "chan"),
        check_vma=False,
    )
```

```python
import functools
import math

import jax
import jax.numpy as jnp
from jax import lax
from jax.experimental import pallas as pl
from jax.experimental.pallas import tpu as pltpu
from jax.sharding import PartitionSpec as P

DEPTHS = 512
TILE_DEV = 1
TILE_BLK = 20
CAP = 6
LANES = 128


floor_value = 0.25
band_mhz = 288.0
depth_step = 32.0


def faraday_table(parts, part_channels, depths):
    channels = parts * part_channels
    chan_index = jnp.arange(channels, dtype=jnp.float32)
    frequency = 800.0 + (chan_index + 0.5) * (band_mhz / channels)
    lambda_sq = 299.792458 / frequency * (299.792458 / frequency)
    shifted = lambda_sq - jnp.mean(lambda_sq)
    depth_grid = (jnp.arange(depths, dtype=jnp.float32) - depths // 2) * depth_step
    phase_angle = 2.0 * depth_grid[:, None] * shifted[None, :]
    cosine = jnp.cos(phase_angle).reshape(depths, parts, part_channels)
    sine_part = jnp.sin(phase_angle).reshape(depths, parts, part_channels)
    real_rows = jnp.stack([cosine, sine_part], axis=2).reshape(depths, 2 * channels)
    imag_rows = jnp.stack([-sine_part, cosine], axis=2).reshape(depths, 2 * channels)
    table = jnp.concatenate([real_rows, imag_rows], axis=0) / jnp.sqrt(jnp.float32(channels))
    return table.astype(jnp.bfloat16)


def in_hbm(array):
    return pltpu.with_memory_space_constraint(array, pltpu.HBM)


def block_groups(count):
    groups, first = [], 0
    while first < count:
        size = min(1 + len(groups), 4, count - first)
        groups.append((first, size))
        first += size
    return groups


def send_body(
    first_tile,
    width,
    obs,
    pattern,
    block_tile,
    correction,
    out,
    tile_s,
    corr_ref,
    corr_rows,
    mix,
    obs_buf,
    pat_buf,
    pat_wide,
    out_buf,
    count,
    in_sem,
    pat_sem,
    out_sem,
    tile_sem,
    corr_sem,
):
    blk_beam, chan_dev, stokes_in, beam_dev, pixels = obs.shape
    beam_count, chan_count = out.shape[:2]
    beams = pattern.shape[1]
    tiles = pixels // chan_count // LANES
    groups = block_groups(blk_beam)
    sides = out_buf.shape[0]
    lanes = width * LANES
    rows = 2 * chan_dev
    beam_row = lax.axis_index("beam")

    def obs_copies(number):
        blocks = pl.ds(*groups[number])
        return [
            pltpu.make_async_copy(
                obs.at[blocks, :, :, :, pl.ds((part * tiles + first_tile + w) * LANES, LANES)],
                obs_buf.at[part * width + w, blocks],
                in_sem.at[number, part * width + w],
            )
            for part in range(chan_count)
            for w in range(width)
        ]

    def out_copy(slot, d, owner, rank):
        return pltpu.make_async_copy(
            out_buf.at[slot, d], out.at[owner, :, rank], out_sem.at[slot, d]
        )

    pat_copies = [
        pltpu.make_async_copy(
            pattern.at[:, :, pl.ds((part * tiles + first_tile) * LANES, lanes)],
            pat_buf.at[part],
            pat_sem.at[part],
        )
        for part in range(chan_count)
    ]
    tile_copy = pltpu.make_async_copy(block_tile, tile_s, tile_sem)
    corr_copy = pltpu.make_async_copy(correction, corr_ref, corr_sem)
    corr_copy.start()
    for copy in obs_copies(0) + pat_copies + [tile_copy]:
        copy.start()
    for number in range(1, len(groups)):
        for copy in obs_copies(number):
            copy.start()

    identity = (
        lax.broadcasted_iota(jnp.int32, (chan_dev, chan_dev), 0)
        == lax.broadcasted_iota(jnp.int32, (chan_dev, chan_dev), 1)
    ).astype(jnp.float32)
    corr_copy.wait()
    for d in range(beam_dev):
        for t in range(stokes_in):
            row = (d * stokes_in + t) * 2
            corr_rows[row : row + 2] = corr_ref[d, t]
    columns = lax.dot_general(
        identity,
        corr_rows[...],
        (((1,), (1,)), ((), ())),
        precision=lax.Precision.HIGHEST,
        preferred_element_type=jnp.float32,
    )
    inner = stokes_in * beam_dev
    wide = (chan_dev, chan_dev * inner)
    offset = lax.broadcasted_iota(jnp.int32, wide, 1) - inner * lax.broadcasted_iota(jnp.int32, wide, 0)
    high, low = [], []
    for d in range(beam_dev):
        for s in range(2):
            block = jnp.zeros(wide, jnp.float32)
            for t in range(stokes_in):
                column = (d * stokes_in + t) * 2 + s
                block = jnp.where(offset == t * beam_dev + d, columns[:, column : column + 1], block)
            top = block.astype(jnp.bfloat16).astype(jnp.float32)
            high.append(top)
            low.append(block - top)
    mix[...] = jnp.concatenate(high + low, axis=0).astype(jnp.bfloat16)

    for owner in range(beam_count):
        count[owner] = 0
    for copy in pat_copies + [tile_copy]:
        copy.wait()
    for part in range(chan_count):
        for w in range(width):
            for k in range(blk_beam):
                pat_wide[part * width + w, k * beams : (k + 1) * beams] = pat_buf[
                    part, k, :, w * LANES : (w + 1) * LANES
                ].astype(jnp.float32)

    def block(k, carry):
        side = lax.rem(k, sides)

        @pl.when(k >= sides)
        def _():
            for d in range(beam_dev):
                out_copy(side, d, 0, 0).wait()

        for first in range(0, chan_count * width, 2):
            observed = jnp.concatenate(
                [obs_buf[first + half, k].reshape(-1, LANES) for half in range(2)], axis=1
            )
            mixed = jnp.dot(mix[...], observed, preferred_element_type=jnp.float32)
            corrected = mixed[: beam_dev * rows] + mixed[beam_dev * rows :]
            for half in range(2):
                part, w = (first + half) // width, (first + half) % width
                for d in range(beam_dev):
                    weight = pat_wide[
                        first + half, pl.ds(k * beams + beam_row * beam_dev + d, 1)
                    ]
                    out_buf[side, d, part, :, w * LANES : (w + 1) * LANES] = (
                        corrected[d * rows : (d + 1) * rows, half * LANES : (half + 1) * LANES] * weight
                    ).astype(jnp.bfloat16)
        for d in range(beam_dev):
            owner = tile_s[beam_row * beam_dev + d, k] // TILE_DEV
            rank = count[owner]
            count[owner] = rank + 1
            out_copy(side, d, owner, rank).start()

        return carry

    for number, (first_block, size) in enumerate(groups):
        for copy in obs_copies(number):
            copy.wait()
        lax.fori_loop(first_block, first_block + size, block, 0)
    for side in range(min(sides, blk_beam)):
        for d in range(beam_dev):
            out_copy(side, d, 0, 0).wait()


def send_chunk(obs_t, pattern_t, block_tile, corr_t, beam_count, chan_count, first_tile, width):
    blk_beam, chan_dev, stokes_in, beam_dev, pixels = obs_t.shape
    rows = chan_dev * 2
    lanes = width * LANES
    beams = pattern_t.shape[1]
    anywhere = pl.BlockSpec(memory_space=pltpu.HBM)
    return pl.pallas_call(
        functools.partial(send_body, first_tile, width),
        out_shape=pltpu.HBM((beam_count, chan_count, CAP, rows, lanes), jnp.bfloat16),
        in_specs=[
            anywhere,
            anywhere,
            anywhere,
            anywhere,
        ],
        out_specs=anywhere,
        scratch_shapes=[
            pltpu.SMEM(block_tile.shape, jnp.int32),
            pltpu.VMEM(corr_t.shape, jnp.float32),
            pltpu.VMEM((corr_t.size // chan_dev, chan_dev), jnp.float32),
            pltpu.VMEM((2 * beam_dev * rows, chan_dev * stokes_in * beam_dev), jnp.bfloat16),
            pltpu.VMEM(
                (chan_count * width, blk_beam, chan_dev, stokes_in, beam_dev, LANES), jnp.bfloat16
            ),
            pltpu.VMEM((chan_count, blk_beam, beams, lanes), jnp.bfloat16),
            pltpu.VMEM((chan_count * width, blk_beam * beams, LANES), jnp.float32),
            pltpu.VMEM((4, beam_dev, chan_count, rows, lanes), jnp.bfloat16),
            pltpu.SMEM((beam_count,), jnp.int32),
            pltpu.SemaphoreType.DMA((len(block_groups(blk_beam)), chan_count * width)),
            pltpu.SemaphoreType.DMA((chan_count,)),
            pltpu.SemaphoreType.DMA((4, beam_dev)),
            pltpu.SemaphoreType.DMA(()),
            pltpu.SemaphoreType.DMA(()),
        ],
        compiler_params=pltpu.CompilerParams(vmem_limit_bytes=61 << 20),
        name=f"send_tile_{first_tile}",
    )(obs_t, in_hbm(pattern_t), in_hbm(block_tile), in_hbm(corr_t))


def sky_body(pair, first_tile, order_s, start_s, recv, inverse_ref, table_ref, *refs):
    out_ref, blocks, total, sem = refs[-4:]
    step = pl.program_id(0)
    parts, rows, lanes = blocks.shape[1:]
    entries = blocks.shape[0]
    slots = pair * pl.num_programs(0)

    def entry_copy(i, source, rank):
        return pltpu.make_async_copy(recv.at[source, :, rank], blocks.at[i], sem.at[i])

    @pl.when(step == 0)
    def _():
        def begin(i, carry):
            entry_copy(i, order_s[0, i], order_s[1, i]).start()
            return carry

        lax.fori_loop(0, start_s[slots], begin, 0)

    for side in range(pair):
        slot = step * pair + side
        columns = slice(side * lanes, (side + 1) * lanes)
        first, last = start_s[slot], start_s[slot + 1]

        @pl.when(first == last)
        def _():
            total[:, columns] = jnp.zeros_like(total[:, columns])

        @pl.when(first < last)
        def _():
            entry_copy(first, 0, 0).wait()
            for part in range(parts):
                total[part * rows : (part + 1) * rows, columns] = blocks[first, part].astype(jnp.float32)

        def add(i, carry):
            entry_copy(i, 0, 0).wait()
            for part in range(parts):
                total[part * rows : (part + 1) * rows, columns] += blocks[i, part].astype(jnp.float32)
            return carry

        lax.fori_loop(first + 1, last, add, 0)
    tiles = lanes // LANES
    sky = jnp.concatenate(
        [
            total[:, tile * LANES : (tile + 1) * LANES]
            * inverse_ref[first_tile + tile % tiles, pl.ds(step * pair + tile // tiles, 1)]
            for tile in range(pair * tiles)
        ],
        axis=1,
    ).astype(jnp.bfloat16)
    piece = math.gcd(table_ref.shape[0], 256)
    for first in range(0, table_ref.shape[0], piece):
        spectrum = jnp.dot(
            table_ref[first : first + piece], sky, preferred_element_type=jnp.float32
        )
        for side in range(pair):
            out_ref[side, first : first + piece] = spectrum[
                :, side * lanes : (side + 1) * lanes
            ].astype(out_ref.dtype)


def sky_chunk(recv, inverse, table, order, start, first_tile, width, tiles, earlier):
    slots = inverse.shape[1]
    pair = math.gcd(slots, 5)
    lanes = width * LANES
    beam_count, parts, capacity, rows = recv.shape[:4]
    anywhere = pl.BlockSpec(memory_space=pltpu.HBM)
    whole = lambda a: pl.BlockSpec(a.shape, lambda l, *s: (0,) * a.ndim)
    in_specs = [anywhere, whole(inverse), whole(table)]
    args = [order, start, in_hbm(recv), inverse, table]
    aliases = {}
    if earlier is not None:
        in_specs.append(anywhere)
        aliases = {len(args): 0}
        args.append(earlier)
    return pl.pallas_call(
        functools.partial(sky_body, pair, first_tile),
        out_shape=jax.ShapeDtypeStruct((slots, table.shape[0], tiles * LANES), jnp.bfloat16),
        grid_spec=pltpu.PrefetchScalarGridSpec(
            num_scalar_prefetch=2,
            grid=(slots // pair,),
            in_specs=in_specs,
            out_specs=pl.BlockSpec(
                (pl.Element(pair), pl.Element(table.shape[0]), pl.Element(lanes)),
                lambda l, *s: (l * pair, 0, first_tile * LANES),
            ),
            scratch_shapes=[
                pltpu.VMEM((beam_count * capacity, parts, rows, lanes), jnp.bfloat16),
                pltpu.VMEM((table.shape[1], pair * lanes), jnp.float32),
                pltpu.SemaphoreType.DMA((beam_count * capacity,)),
            ],
        ),
        input_output_aliases=aliases,
        compiler_params=pltpu.CompilerParams(vmem_limit_bytes=48 << 20),
        name=f"sky_tile_{first_tile}",
    )(*args)


def received_order(block_tile, block_offset, beam_row, beam_count, beam_dev, blk_beam):
    local_slots = TILE_DEV * TILE_BLK

    def by_block(a):
        return jnp.swapaxes(a.reshape(beam_count, beam_dev, blk_beam), 1, 2).reshape(beam_count, -1)

    tile = by_block(block_tile)
    slot_of = tile % TILE_DEV * TILE_BLK + by_block(block_offset)
    mine = tile // TILE_DEV == beam_row
    position = jnp.arange(beam_dev * blk_beam, dtype=jnp.int32)
    earlier = position[None, :] < position[:, None]
    rank_in = jnp.sum((mine[:, None, :] & earlier[None]).astype(jnp.int32), axis=2)
    ranks = jnp.arange(CAP, dtype=jnp.int32)
    hit = mine[:, :, None] & (rank_in[:, :, None] == ranks[None, None, :])
    entry_slot = jnp.min(jnp.where(hit, slot_of[:, :, None], local_slots), axis=1).reshape(-1)
    index = jnp.arange(beam_count * CAP, dtype=jnp.int32)
    before = (entry_slot[None, :] < entry_slot[:, None]) | (
        (entry_slot[None, :] == entry_slot[:, None]) & (index[None, :] < index[:, None])
    )
    place = jnp.sum(before.astype(jnp.int32), axis=1)
    order = jnp.sum(jnp.where(place[None, :] == index[:, None], index[None, :], 0), axis=1)
    slot_index = jnp.arange(local_slots + 1, dtype=jnp.int32)
    start = jnp.sum((entry_slot[None, :] < slot_index[:, None]).astype(jnp.int32), axis=1)
    return jnp.stack([order // CAP, order % CAP]), start


def pixel_chunks(tiles):
    if tiles < 4:
        return [(tile, 1) for tile in range(tiles)]
    return [(0, 1), (1, tiles - 2), (tiles - 1, 1)]


def shards(observed, beam_pattern, correction, block_tile, block_offset):
    beam_count = lax.axis_size("beam")
    chan_count = lax.axis_size("chan")
    beam_row = lax.axis_index("beam")
    chan_part = lax.axis_index("chan")
    beam_dev, blk_beam, chan_dev, stokes_in, pixels = observed.shape
    pixel_share = pixels // chan_count
    tiles = pixel_share // LANES
    local_slots = TILE_DEV * TILE_BLK

    obs_t = jnp.transpose(observed, (1, 2, 3, 0, 4))
    pattern_t = jnp.transpose(beam_pattern, (1, 0, 2))
    corr_t = jnp.transpose(correction, (0, 3, 2, 1))

    order, start = received_order(
        block_tile, block_offset, beam_row, beam_count, beam_dev, blk_beam
    )
    global_slot = (block_tile * TILE_BLK + block_offset).reshape(-1)
    slot_range = beam_row * local_slots + jnp.arange(local_slots, dtype=jnp.int32)
    cover = (global_slot[None, :] == slot_range[:, None]).astype(jnp.float32)
    share = lax.dynamic_slice_in_dim(beam_pattern, chan_part * pixel_share, pixel_share, 2)
    share = share.astype(jnp.float32).reshape(-1, pixel_share)
    weight_sum = jnp.dot(cover, share * share, precision=lax.Precision.HIGHEST)
    inverse = 1.0 / jnp.maximum(weight_sum, floor_value)
    inverse = jnp.swapaxes(inverse.reshape(local_slots, tiles, LANES), 0, 1)
    table = faraday_table(chan_count, chan_dev, DEPTHS)

    spectrum = None
    for first_tile, width in pixel_chunks(tiles):
        sent = send_chunk(
            obs_t, pattern_t, block_tile, corr_t, beam_count, chan_count, first_tile, width
        )
        received = lax.all_to_all(
            sent.reshape((beam_count * chan_count,) + sent.shape[2:]),
            ("beam", "chan"),
            split_axis=0,
            concat_axis=0,
            tiled=True,
        ).reshape(sent.shape)
        spectrum = sky_chunk(
            received,
            inverse,
            table,
            order,
            start,
            first_tile,
            width,
            tiles,
            spectrum,
        )
    return spectrum.reshape(TILE_DEV, TILE_BLK, 2, DEPTHS, pixel_share)


def solution(mesh):
    placed = (P("beam", None, "chan", None, None), P(), P("beam", "chan", None, None), P(), P())
    return jax.shard_map(
        shards,
        mesh=mesh,
        in_specs=placed,
        out_specs=P("beam", None, None, None, "chan"),
        check_vma=False,
    )
```

```python
import functools
import math

import jax
import jax.numpy as jnp
from jax import lax
from jax.experimental import pallas as pl
from jax.experimental.pallas import tpu as pltpu
from jax.sharding import PartitionSpec as P

DEPTHS = 512
TILE_DEV = 1
TILE_BLK = 20
CAP = 6
LANES = 128


floor_value = 0.25
band_mhz = 288.0
depth_step = 32.0


def faraday_table(parts, part_channels, depths):
    channels = parts * part_channels
    chan_index = jnp.arange(channels, dtype=jnp.float32)
    frequency = 800.0 + (chan_index + 0.5) * (band_mhz / channels)
    lambda_sq = 299.792458 / frequency * (299.792458 / frequency)
    shifted = lambda_sq - jnp.mean(lambda_sq)
    depth_grid = (jnp.arange(depths, dtype=jnp.float32) - depths // 2) * depth_step
    phase_angle = 2.0 * depth_grid[:, None] * shifted[None, :]
    cosine = jnp.cos(phase_angle).reshape(depths, parts, part_channels)
    sine_part = jnp.sin(phase_angle).reshape(depths, parts, part_channels)
    real_rows = jnp.stack([cosine, sine_part], axis=2).reshape(depths, 2 * channels)
    imag_rows = jnp.stack([-sine_part, cosine], axis=2).reshape(depths, 2 * channels)
    table = jnp.concatenate([real_rows, imag_rows], axis=0) / jnp.sqrt(jnp.float32(channels))
    return table.astype(jnp.bfloat16)


def in_hbm(array):
    return pltpu.with_memory_space_constraint(array, pltpu.HBM)


def block_groups(count):
    groups, first = [], 0
    while first < count:
        size = min(2 + len(groups), 6, count - first)
        groups.append((first, size))
        first += size
    return groups


def send_body(
    first_tile,
    width,
    obs,
    pattern,
    block_tile,
    correction,
    out,
    tile_s,
    corr_ref,
    corr_rows,
    mix,
    obs_buf,
    pat_buf,
    pat_wide,
    out_buf,
    count,
    in_sem,
    pat_sem,
    out_sem,
    tile_sem,
    corr_sem,
):
    blk_beam, chan_dev, stokes_in, beam_dev, pixels = obs.shape
    chan_count, beam_count = out.shape[:2]
    beams = pattern.shape[1]
    tiles = pixels // chan_count // LANES
    groups = block_groups(blk_beam)
    sides = out_buf.shape[0]
    lanes = width * LANES
    rows = 2 * chan_dev
    beam_row = lax.axis_index("beam")

    def obs_copies(number):
        blocks = pl.ds(*groups[number])
        return [
            pltpu.make_async_copy(
                obs.at[blocks, :, :, :, pl.ds((part * tiles + first_tile + w) * LANES, LANES)],
                obs_buf.at[part * width + w, blocks],
                in_sem.at[number, part * width + w],
            )
            for part in range(chan_count)
            for w in range(width)
        ]

    def out_copy(slot, d, owner, rank):
        return pltpu.make_async_copy(
            out_buf.at[slot, d], out.at[:, owner, rank], out_sem.at[slot, d]
        )

    pat_copies = [
        pltpu.make_async_copy(
            pattern.at[:, :, pl.ds((part * tiles + first_tile) * LANES, lanes)],
            pat_buf.at[part],
            pat_sem.at[part],
        )
        for part in range(chan_count)
    ]
    tile_copy = pltpu.make_async_copy(block_tile, tile_s, tile_sem)
    corr_copy = pltpu.make_async_copy(correction, corr_ref, corr_sem)
    corr_copy.start()
    for copy in obs_copies(0) + pat_copies + [tile_copy]:
        copy.start()
    for number in range(1, len(groups)):
        for copy in obs_copies(number):
            copy.start()

    identity = (
        lax.broadcasted_iota(jnp.int32, (chan_dev, chan_dev), 0)
        == lax.broadcasted_iota(jnp.int32, (chan_dev, chan_dev), 1)
    ).astype(jnp.float32)
    corr_copy.wait()
    for d in range(beam_dev):
        for t in range(stokes_in):
            row = (d * stokes_in + t) * 2
            corr_rows[row : row + 2] = corr_ref[d, t]
    columns = lax.dot_general(
        identity,
        corr_rows[...],
        (((1,), (1,)), ((), ())),
        precision=lax.Precision.HIGHEST,
        preferred_element_type=jnp.float32,
    )
    inner = stokes_in * beam_dev
    wide = (chan_dev, chan_dev * inner)
    offset = lax.broadcasted_iota(jnp.int32, wide, 1) - inner * lax.broadcasted_iota(jnp.int32, wide, 0)
    high, low = [], []
    for d in range(beam_dev):
        for s in range(2):
            block = jnp.zeros(wide, jnp.float32)
            for t in range(stokes_in):
                column = (d * stokes_in + t) * 2 + s
                block = jnp.where(offset == t * beam_dev + d, columns[:, column : column + 1], block)
            top = block.astype(jnp.bfloat16).astype(jnp.float32)
            high.append(top)
            low.append(block - top)
    mix[...] = jnp.concatenate(high + low, axis=0).astype(jnp.bfloat16)

    for owner in range(beam_count):
        count[owner] = 0
    for copy in pat_copies + [tile_copy]:
        copy.wait()
    for part in range(chan_count):
        for w in range(width):
            for k in range(blk_beam):
                pat_wide[part * width + w, k * beams : (k + 1) * beams] = pat_buf[
                    part, k, :, w * LANES : (w + 1) * LANES
                ].astype(jnp.float32)

    def block(k, carry):
        side = lax.rem(k, sides)

        @pl.when(k >= sides)
        def _():
            for d in range(beam_dev):
                out_copy(side, d, 0, 0).wait()

        for first in range(0, chan_count * width, 2):
            observed = jnp.concatenate(
                [obs_buf[first + half, k].reshape(-1, LANES) for half in range(2)], axis=1
            )
            mixed = jnp.dot(mix[...], observed, preferred_element_type=jnp.float32)
            corrected = mixed[: beam_dev * rows] + mixed[beam_dev * rows :]
            for half in range(2):
                part, w = (first + half) // width, (first + half) % width
                for d in range(beam_dev):
                    weight = pat_wide[
                        first + half, pl.ds(k * beams + beam_row * beam_dev + d, 1)
                    ]
                    out_buf[side, d, part, :, w * LANES : (w + 1) * LANES] = (
                        corrected[d * rows : (d + 1) * rows, half * LANES : (half + 1) * LANES] * weight
                    ).astype(jnp.bfloat16)
        for d in range(beam_dev):
            owner = tile_s[beam_row * beam_dev + d, k] // TILE_DEV
            rank = count[owner]
            count[owner] = rank + 1
            out_copy(side, d, owner, rank).start()

        return carry

    for number, (first_block, size) in enumerate(groups):
        for copy in obs_copies(number):
            copy.wait()
        lax.fori_loop(first_block, first_block + size, block, 0)
    for side in range(min(sides, blk_beam)):
        for d in range(beam_dev):
            out_copy(side, d, 0, 0).wait()


def send_chunk(obs_t, pattern_t, block_tile, corr_t, beam_count, chan_count, first_tile, width):
    blk_beam, chan_dev, stokes_in, beam_dev, pixels = obs_t.shape
    rows = chan_dev * 2
    lanes = width * LANES
    beams = pattern_t.shape[1]
    anywhere = pl.BlockSpec(memory_space=pltpu.HBM)
    return pl.pallas_call(
        functools.partial(send_body, first_tile, width),
        out_shape=pltpu.HBM((chan_count, beam_count, CAP, rows, lanes), jnp.bfloat16),
        in_specs=[
            anywhere,
            anywhere,
            anywhere,
            anywhere,
        ],
        out_specs=anywhere,
        scratch_shapes=[
            pltpu.SMEM(block_tile.shape, jnp.int32),
            pltpu.VMEM(corr_t.shape, jnp.float32),
            pltpu.VMEM((corr_t.size // chan_dev, chan_dev), jnp.float32),
            pltpu.VMEM((2 * beam_dev * rows, chan_dev * stokes_in * beam_dev), jnp.bfloat16),
            pltpu.VMEM(
                (chan_count * width, blk_beam, chan_dev, stokes_in, beam_dev, LANES), jnp.bfloat16
            ),
            pltpu.VMEM((chan_count, blk_beam, beams, lanes), jnp.bfloat16),
            pltpu.VMEM((chan_count * width, blk_beam * beams, LANES), jnp.float32),
            pltpu.VMEM((4, beam_dev, chan_count, rows, lanes), jnp.bfloat16),
            pltpu.SMEM((beam_count,), jnp.int32),
            pltpu.SemaphoreType.DMA((len(block_groups(blk_beam)), chan_count * width)),
            pltpu.SemaphoreType.DMA((chan_count,)),
            pltpu.SemaphoreType.DMA((4, beam_dev)),
            pltpu.SemaphoreType.DMA(()),
            pltpu.SemaphoreType.DMA(()),
        ],
        compiler_params=pltpu.CompilerParams(vmem_limit_bytes=61 << 20),
        name=f"send_tile_{first_tile}",
    )(obs_t, in_hbm(pattern_t), in_hbm(block_tile), in_hbm(corr_t))


def sky_body(pair, first_tile, order_s, start_s, recv, inverse_ref, table_ref, *refs):
    out_ref, blocks, total, sem = refs[-4:]
    step = pl.program_id(0)
    parts, rows, lanes = blocks.shape[1:]
    entries = blocks.shape[0]
    slots = pair * pl.num_programs(0)

    def entry_copy(i, source, rank):
        return pltpu.make_async_copy(recv.at[:, source, rank], blocks.at[i], sem.at[i])

    @pl.when(step == 0)
    def _():
        def begin(i, carry):
            entry_copy(i, order_s[0, i], order_s[1, i]).start()
            return carry

        lax.fori_loop(0, start_s[slots], begin, 0)

    for side in range(pair):
        slot = step * pair + side
        columns = slice(side * lanes, (side + 1) * lanes)
        first, last = start_s[slot], start_s[slot + 1]

        @pl.when(first == last)
        def _():
            total[:, columns] = jnp.zeros_like(total[:, columns])

        @pl.when(first < last)
        def _():
            entry_copy(first, 0, 0).wait()
            for part in range(parts):
                total[part * rows : (part + 1) * rows, columns] = blocks[first, part].astype(jnp.float32)

        def add(i, carry):
            entry_copy(i, 0, 0).wait()
            for part in range(parts):
                total[part * rows : (part + 1) * rows, columns] += blocks[i, part].astype(jnp.float32)
            return carry

        lax.fori_loop(first + 1, last, add, 0)
    tiles = lanes // LANES
    sky = jnp.concatenate(
        [
            total[:, tile * LANES : (tile + 1) * LANES]
            * inverse_ref[first_tile + tile % tiles, pl.ds(step * pair + tile // tiles, 1)]
            for tile in range(pair * tiles)
        ],
        axis=1,
    ).astype(jnp.bfloat16)
    piece = math.gcd(table_ref.shape[0], 256)
    for first in range(0, table_ref.shape[0], piece):
        spectrum = jnp.dot(
            table_ref[first : first + piece], sky, preferred_element_type=jnp.float32
        )
        for side in range(pair):
            out_ref[side, first : first + piece] = spectrum[
                :, side * lanes : (side + 1) * lanes
            ].astype(out_ref.dtype)


def sky_chunk(recv, inverse, table, order, start, first_tile, width, tiles, earlier):
    slots = inverse.shape[1]
    pair = math.gcd(slots, 5)
    lanes = width * LANES
    parts, beam_count, capacity, rows = recv.shape[:4]
    anywhere = pl.BlockSpec(memory_space=pltpu.HBM)
    whole = lambda a: pl.BlockSpec(a.shape, lambda l, *s: (0,) * a.ndim)
    in_specs = [anywhere, whole(inverse), whole(table)]
    args = [order, start, in_hbm(recv), inverse, table]
    aliases = {}
    if earlier is not None:
        in_specs.append(anywhere)
        aliases = {len(args): 0}
        args.append(earlier)
    return pl.pallas_call(
        functools.partial(sky_body, pair, first_tile),
        out_shape=jax.ShapeDtypeStruct((slots, table.shape[0], tiles * LANES), jnp.bfloat16),
        grid_spec=pltpu.PrefetchScalarGridSpec(
            num_scalar_prefetch=2,
            grid=(slots // pair,),
            in_specs=in_specs,
            out_specs=pl.BlockSpec(
                (pl.Element(pair), pl.Element(table.shape[0]), pl.Element(lanes)),
                lambda l, *s: (l * pair, 0, first_tile * LANES),
            ),
            scratch_shapes=[
                pltpu.VMEM((beam_count * capacity, parts, rows, lanes), jnp.bfloat16),
                pltpu.VMEM((table.shape[1], pair * lanes), jnp.float32),
                pltpu.SemaphoreType.DMA((beam_count * capacity,)),
            ],
        ),
        input_output_aliases=aliases,
        compiler_params=pltpu.CompilerParams(vmem_limit_bytes=48 << 20),
        name=f"sky_tile_{first_tile}",
    )(*args)


def received_order(block_tile, block_offset, beam_row, beam_count, beam_dev, blk_beam):
    local_slots = TILE_DEV * TILE_BLK

    def by_block(a):
        return jnp.swapaxes(a.reshape(beam_count, beam_dev, blk_beam), 1, 2).reshape(beam_count, -1)

    tile = by_block(block_tile)
    slot_of = tile % TILE_DEV * TILE_BLK + by_block(block_offset)
    mine = tile // TILE_DEV == beam_row
    position = jnp.arange(beam_dev * blk_beam, dtype=jnp.int32)
    earlier = position[None, :] < position[:, None]
    rank_in = jnp.sum((mine[:, None, :] & earlier[None]).astype(jnp.int32), axis=2)
    ranks = jnp.arange(CAP, dtype=jnp.int32)
    hit = mine[:, :, None] & (rank_in[:, :, None] == ranks[None, None, :])
    entry_slot = jnp.min(jnp.where(hit, slot_of[:, :, None], local_slots), axis=1).reshape(-1)
    index = jnp.arange(beam_count * CAP, dtype=jnp.int32)
    before = (entry_slot[None, :] < entry_slot[:, None]) | (
        (entry_slot[None, :] == entry_slot[:, None]) & (index[None, :] < index[:, None])
    )
    place = jnp.sum(before.astype(jnp.int32), axis=1)
    order = jnp.sum(jnp.where(place[None, :] == index[:, None], index[None, :], 0), axis=1)
    slot_index = jnp.arange(local_slots + 1, dtype=jnp.int32)
    start = jnp.sum((entry_slot[None, :] < slot_index[:, None]).astype(jnp.int32), axis=1)
    return jnp.stack([order // CAP, order % CAP]), start


def pixel_chunks(tiles):
    if tiles < 4:
        return [(tile, 1) for tile in range(tiles)]
    return [(0, 1), (1, tiles - 2), (tiles - 1, 1)]


def shards(observed, beam_pattern, correction, block_tile, block_offset):
    beam_count = lax.axis_size("beam")
    chan_count = lax.axis_size("chan")
    beam_row = lax.axis_index("beam")
    chan_part = lax.axis_index("chan")
    beam_dev, blk_beam, chan_dev, stokes_in, pixels = observed.shape
    pixel_share = pixels // chan_count
    tiles = pixel_share // LANES
    local_slots = TILE_DEV * TILE_BLK

    obs_t = jnp.transpose(observed, (1, 2, 3, 0, 4))
    pattern_t = jnp.transpose(beam_pattern, (1, 0, 2))
    corr_t = jnp.transpose(correction, (0, 3, 2, 1))

    order, start = received_order(
        block_tile, block_offset, beam_row, beam_count, beam_dev, blk_beam
    )
    global_slot = (block_tile * TILE_BLK + block_offset).reshape(-1)
    slot_range = beam_row * local_slots + jnp.arange(local_slots, dtype=jnp.int32)
    cover = (global_slot[None, :] == slot_range[:, None]).astype(jnp.float32)
    share = lax.dynamic_slice_in_dim(beam_pattern, chan_part * pixel_share, pixel_share, 2)
    share = share.astype(jnp.float32).reshape(-1, pixel_share)
    weight_sum = jnp.dot(cover, share * share, precision=lax.Precision.HIGHEST)
    inverse = 1.0 / jnp.maximum(weight_sum, floor_value)
    inverse = jnp.swapaxes(inverse.reshape(local_slots, tiles, LANES), 0, 1)
    table = faraday_table(chan_count, chan_dev, DEPTHS)

    spectrum = None
    for first_tile, width in pixel_chunks(tiles):
        sent = send_chunk(
            obs_t, pattern_t, block_tile, corr_t, beam_count, chan_count, first_tile, width
        )
        received = lax.all_to_all(
            sent.reshape((chan_count * beam_count,) + sent.shape[2:]),
            ("chan", "beam"),
            split_axis=0,
            concat_axis=0,
            tiled=True,
        ).reshape(sent.shape)
        spectrum = sky_chunk(
            received,
            inverse,
            table,
            order,
            start,
            first_tile,
            width,
            tiles,
            spectrum,
        )
    return spectrum.reshape(TILE_DEV, TILE_BLK, 2, DEPTHS, pixel_share)


def solution(mesh):
    placed = (P("beam", None, "chan", None, None), P(), P("beam", "chan", None, None), P(), P())
    return jax.shard_map(
        shards,
        mesh=mesh,
        in_specs=placed,
        out_specs=P("beam", None, None, None, "chan"),
        check_vma=False,
    )
```

```python
import functools
import math

import jax
import jax.numpy as jnp
from jax import lax
from jax.experimental import pallas as pl
from jax.experimental.pallas import tpu as pltpu
from jax.sharding import PartitionSpec as P

DEPTHS = 512
TILE_DEV = 1
TILE_BLK = 20
CAP = 6
LANES = 128


floor_value = 0.25
band_mhz = 288.0
depth_step = 32.0


def faraday_table(parts, part_channels, depths):
    channels = parts * part_channels
    chan_index = jnp.arange(channels, dtype=jnp.float32)
    frequency = 800.0 + (chan_index + 0.5) * (band_mhz / channels)
    lambda_sq = 299.792458 / frequency * (299.792458 / frequency)
    shifted = lambda_sq - jnp.mean(lambda_sq)
    depth_grid = (jnp.arange(depths, dtype=jnp.float32) - depths // 2) * depth_step
    phase_angle = 2.0 * depth_grid[:, None] * shifted[None, :]
    cosine = jnp.cos(phase_angle).reshape(depths, parts, part_channels)
    sine_part = jnp.sin(phase_angle).reshape(depths, parts, part_channels)
    real_rows = jnp.stack([cosine, sine_part], axis=2).reshape(depths, 2 * channels)
    imag_rows = jnp.stack([-sine_part, cosine], axis=2).reshape(depths, 2 * channels)
    table = jnp.concatenate([real_rows, imag_rows], axis=0) / jnp.sqrt(jnp.float32(channels))
    return table.astype(jnp.bfloat16)


def in_hbm(array):
    return pltpu.with_memory_space_constraint(array, pltpu.HBM)


def block_groups(count):
    groups, first = [], 0
    while first < count:
        size = min(2 + len(groups), 6, count - first)
        groups.append((first, size))
        first += size
    return groups


def send_body(
    first_tile,
    width,
    obs,
    pattern,
    block_tile,
    correction,
    out,
    tile_s,
    corr_ref,
    corr_rows,
    mix,
    obs_buf,
    pat_buf,
    pat_wide,
    out_buf,
    count,
    in_sem,
    pat_sem,
    out_sem,
    tile_sem,
    corr_sem,
):
    blk_beam, chan_dev, stokes_in, beam_dev, pixels = obs.shape
    chan_count, beam_count = out.shape[:2]
    beams = pattern.shape[1]
    tiles = pixels // chan_count // LANES
    groups = block_groups(blk_beam)
    sides = out_buf.shape[0]
    lanes = width * LANES
    rows = 2 * chan_dev
    beam_row = lax.axis_index("beam")

    def obs_copies(number):
        blocks = pl.ds(*groups[number])
        return [
            pltpu.make_async_copy(
                obs.at[blocks, :, :, :, pl.ds((part * tiles + first_tile + w) * LANES, LANES)],
                obs_buf.at[part * width + w, blocks],
                in_sem.at[number, part * width + w],
            )
            for part in range(chan_count)
            for w in range(width)
        ]

    def out_copy(slot, d, owner, rank):
        return pltpu.make_async_copy(
            out_buf.at[slot, d], out.at[:, owner, rank], out_sem.at[slot, d]
        )

    pat_copies = [
        pltpu.make_async_copy(
            pattern.at[:, :, pl.ds((part * tiles + first_tile) * LANES, lanes)],
            pat_buf.at[part],
            pat_sem.at[part],
        )
        for part in range(chan_count)
    ]
    tile_copy = pltpu.make_async_copy(block_tile, tile_s, tile_sem)
    corr_copy = pltpu.make_async_copy(correction, corr_ref, corr_sem)
    corr_copy.start()
    for copy in obs_copies(0) + pat_copies + [tile_copy]:
        copy.start()
    for number in range(1, len(groups)):
        for copy in obs_copies(number):
            copy.start()

    identity = (
        lax.broadcasted_iota(jnp.int32, (chan_dev, chan_dev), 0)
        == lax.broadcasted_iota(jnp.int32, (chan_dev, chan_dev), 1)
    ).astype(jnp.float32)
    corr_copy.wait()
    for d in range(beam_dev):
        for t in range(stokes_in):
            row = (d * stokes_in + t) * 2
            corr_rows[row : row + 2] = corr_ref[d, t]
    columns = lax.dot_general(
        identity,
        corr_rows[...],
        (((1,), (1,)), ((), ())),
        precision=lax.Precision.HIGHEST,
        preferred_element_type=jnp.float32,
    )
    inner = stokes_in * beam_dev
    wide = (chan_dev, chan_dev * inner)
    offset = lax.broadcasted_iota(jnp.int32, wide, 1) - inner * lax.broadcasted_iota(jnp.int32, wide, 0)
    high, low = [], []
    for d in range(beam_dev):
        for s in range(2):
            block = jnp.zeros(wide, jnp.float32)
            for t in range(stokes_in):
                column = (d * stokes_in + t) * 2 + s
                block = jnp.where(offset == t * beam_dev + d, columns[:, column : column + 1], block)
            top = block.astype(jnp.bfloat16).astype(jnp.float32)
            high.append(top)
            low.append(block - top)
    mix[...] = jnp.concatenate(high + low, axis=0).astype(jnp.bfloat16)

    for owner in range(beam_count):
        count[owner] = 0
    for copy in pat_copies + [tile_copy]:
        copy.wait()
    for part in range(chan_count):
        for w in range(width):
            for k in range(blk_beam):
                pat_wide[part * width + w, k * beams : (k + 1) * beams] = pat_buf[
                    part, k, :, w * LANES : (w + 1) * LANES
                ].astype(jnp.float32)

    def block(k, carry):
        side = lax.rem(k, sides)

        @pl.when(k >= sides)
        def _():
            for d in range(beam_dev):
                out_copy(side, d, 0, 0).wait()

        for first in range(0, chan_count * width, 2):
            observed = jnp.concatenate(
                [obs_buf[first + half, k].reshape(-1, LANES) for half in range(2)], axis=1
            )
            mixed = jnp.dot(mix[...], observed, preferred_element_type=jnp.float32)
            corrected = mixed[: beam_dev * rows] + mixed[beam_dev * rows :]
            for half in range(2):
                part, w = (first + half) // width, (first + half) % width
                for d in range(beam_dev):
                    weight = pat_wide[
                        first + half, pl.ds(k * beams + beam_row * beam_dev + d, 1)
                    ]
                    out_buf[side, d, part, :, w * LANES : (w + 1) * LANES] = (
                        corrected[d * rows : (d + 1) * rows, half * LANES : (half + 1) * LANES] * weight
                    ).astype(jnp.bfloat16)
        for d in range(beam_dev):
            owner = tile_s[beam_row * beam_dev + d, k] // TILE_DEV
            rank = count[owner]
            count[owner] = rank + 1
            out_copy(side, d, owner, rank).start()

        return carry

    for number, (first_block, size) in enumerate(groups):
        for copy in obs_copies(number):
            copy.wait()
        lax.fori_loop(first_block, first_block + size, block, 0)
    for side in range(min(sides, blk_beam)):
        for d in range(beam_dev):
            out_copy(side, d, 0, 0).wait()


def send_chunk(obs_t, pattern_t, block_tile, corr_t, beam_count, chan_count, first_tile, width):
    blk_beam, chan_dev, stokes_in, beam_dev, pixels = obs_t.shape
    rows = chan_dev * 2
    lanes = width * LANES
    beams = pattern_t.shape[1]
    anywhere = pl.BlockSpec(memory_space=pltpu.HBM)
    return pl.pallas_call(
        functools.partial(send_body, first_tile, width),
        out_shape=pltpu.HBM((chan_count, beam_count, CAP, rows, lanes), jnp.bfloat16),
        in_specs=[
            anywhere,
            anywhere,
            anywhere,
            anywhere,
        ],
        out_specs=anywhere,
        scratch_shapes=[
            pltpu.SMEM(block_tile.shape, jnp.int32),
            pltpu.VMEM(corr_t.shape, jnp.float32),
            pltpu.VMEM((corr_t.size // chan_dev, chan_dev), jnp.float32),
            pltpu.VMEM((2 * beam_dev * rows, chan_dev * stokes_in * beam_dev), jnp.bfloat16),
            pltpu.VMEM(
                (chan_count * width, blk_beam, chan_dev, stokes_in, beam_dev, LANES), jnp.bfloat16
            ),
            pltpu.VMEM((chan_count, blk_beam, beams, lanes), jnp.bfloat16),
            pltpu.VMEM((chan_count * width, blk_beam * beams, LANES), jnp.float32),
            pltpu.VMEM((4, beam_dev, chan_count, rows, lanes), jnp.bfloat16),
            pltpu.SMEM((beam_count,), jnp.int32),
            pltpu.SemaphoreType.DMA((len(block_groups(blk_beam)), chan_count * width)),
            pltpu.SemaphoreType.DMA((chan_count,)),
            pltpu.SemaphoreType.DMA((4, beam_dev)),
            pltpu.SemaphoreType.DMA(()),
            pltpu.SemaphoreType.DMA(()),
        ],
        compiler_params=pltpu.CompilerParams(vmem_limit_bytes=61 << 20),
        name=f"send_tile_{first_tile}",
    )(obs_t, in_hbm(pattern_t), in_hbm(block_tile), in_hbm(corr_t))


def sky_body(pair, first_tile, order_s, start_s, recv, inverse_ref, table_ref, *refs):
    out_ref, blocks, total, sem = refs[-4:]
    step = pl.program_id(0)
    parts, rows, lanes = blocks.shape[1:]
    entries = blocks.shape[0]
    slots = pair * pl.num_programs(0)

    def entry_copy(i, source, rank):
        return pltpu.make_async_copy(recv.at[:, source, rank], blocks.at[i], sem.at[i])

    @pl.when(step == 0)
    def _():
        def begin(i, carry):
            entry_copy(i, order_s[0, i], order_s[1, i]).start()
            return carry

        lax.fori_loop(0, start_s[slots], begin, 0)

    for side in range(pair):
        slot = step * pair + side
        columns = slice(side * lanes, (side + 1) * lanes)
        first, last = start_s[slot], start_s[slot + 1]

        @pl.when(first == last)
        def _():
            total[:, columns] = jnp.zeros_like(total[:, columns])

        @pl.when(first < last)
        def _():
            entry_copy(first, 0, 0).wait()
            for part in range(parts):
                total[part * rows : (part + 1) * rows, columns] = blocks[first, part].astype(jnp.float32)

        def add(i, carry):
            entry_copy(i, 0, 0).wait()
            for part in range(parts):
                total[part * rows : (part + 1) * rows, columns] += blocks[i, part].astype(jnp.float32)
            return carry

        lax.fori_loop(first + 1, last, add, 0)
    tiles = lanes // LANES
    sky = jnp.concatenate(
        [
            total[:, tile * LANES : (tile + 1) * LANES]
            * inverse_ref[first_tile + tile % tiles, pl.ds(step * pair + tile // tiles, 1)]
            for tile in range(pair * tiles)
        ],
        axis=1,
    ).astype(jnp.bfloat16)
    piece = math.gcd(table_ref.shape[0], 512)
    for first in range(0, table_ref.shape[0], piece):
        spectrum = jnp.dot(
            table_ref[first : first + piece], sky, preferred_element_type=jnp.float32
        )
        for side in range(pair):
            out_ref[side, first : first + piece] = spectrum[
                :, side * lanes : (side + 1) * lanes
            ].astype(out_ref.dtype)


def sky_chunk(recv, inverse, table, order, start, first_tile, width, tiles, earlier):
    slots = inverse.shape[1]
    pair = math.gcd(slots, 10 if width == 1 else 5)
    lanes = width * LANES
    parts, beam_count, capacity, rows = recv.shape[:4]
    anywhere = pl.BlockSpec(memory_space=pltpu.HBM)
    whole = lambda a: pl.BlockSpec(a.shape, lambda l, *s: (0,) * a.ndim)
    in_specs = [anywhere, whole(inverse), whole(table)]
    args = [order, start, in_hbm(recv), inverse, table]
    aliases = {}
    if earlier is not None:
        in_specs.append(anywhere)
        aliases = {len(args): 0}
        args.append(earlier)
    return pl.pallas_call(
        functools.partial(sky_body, pair, first_tile),
        out_shape=jax.ShapeDtypeStruct((slots, table.shape[0], tiles * LANES), jnp.bfloat16),
        grid_spec=pltpu.PrefetchScalarGridSpec(
            num_scalar_prefetch=2,
            grid=(slots // pair,),
            in_specs=in_specs,
            out_specs=pl.BlockSpec(
                (pl.Element(pair), pl.Element(table.shape[0]), pl.Element(lanes)),
                lambda l, *s: (l * pair, 0, first_tile * LANES),
            ),
            scratch_shapes=[
                pltpu.VMEM((beam_count * capacity, parts, rows, lanes), jnp.bfloat16),
                pltpu.VMEM((table.shape[1], pair * lanes), jnp.float32),
                pltpu.SemaphoreType.DMA((beam_count * capacity,)),
            ],
        ),
        input_output_aliases=aliases,
        compiler_params=pltpu.CompilerParams(vmem_limit_bytes=48 << 20),
        name=f"sky_tile_{first_tile}",
    )(*args)


def received_order(block_tile, block_offset, beam_row, beam_count, beam_dev, blk_beam):
    local_slots = TILE_DEV * TILE_BLK

    def by_block(a):
        return jnp.swapaxes(a.reshape(beam_count, beam_dev, blk_beam), 1, 2).reshape(beam_count, -1)

    tile = by_block(block_tile)
    slot_of = tile % TILE_DEV * TILE_BLK + by_block(block_offset)
    mine = tile // TILE_DEV == beam_row
    position = jnp.arange(beam_dev * blk_beam, dtype=jnp.int32)
    earlier = position[None, :] < position[:, None]
    rank_in = jnp.sum((mine[:, None, :] & earlier[None]).astype(jnp.int32), axis=2)
    ranks = jnp.arange(CAP, dtype=jnp.int32)
    hit = mine[:, :, None] & (rank_in[:, :, None] == ranks[None, None, :])
    entry_slot = jnp.min(jnp.where(hit, slot_of[:, :, None], local_slots), axis=1).reshape(-1)
    index = jnp.arange(beam_count * CAP, dtype=jnp.int32)
    before = (entry_slot[None, :] < entry_slot[:, None]) | (
        (entry_slot[None, :] == entry_slot[:, None]) & (index[None, :] < index[:, None])
    )
    place = jnp.sum(before.astype(jnp.int32), axis=1)
    order = jnp.sum(jnp.where(place[None, :] == index[:, None], index[None, :], 0), axis=1)
    slot_index = jnp.arange(local_slots + 1, dtype=jnp.int32)
    start = jnp.sum((entry_slot[None, :] < slot_index[:, None]).astype(jnp.int32), axis=1)
    return jnp.stack([order // CAP, order % CAP]), start


def pixel_chunks(tiles):
    if tiles < 4:
        return [(tile, 1) for tile in range(tiles)]
    return [(0, 1), (1, tiles - 2), (tiles - 1, 1)]


def shards(observed, beam_pattern, correction, block_tile, block_offset):
    beam_count = lax.axis_size("beam")
    chan_count = lax.axis_size("chan")
    beam_row = lax.axis_index("beam")
    chan_part = lax.axis_index("chan")
    beam_dev, blk_beam, chan_dev, stokes_in, pixels = observed.shape
    pixel_share = pixels // chan_count
    tiles = pixel_share // LANES
    local_slots = TILE_DEV * TILE_BLK

    obs_t = jnp.transpose(observed, (1, 2, 3, 0, 4))
    pattern_t = jnp.transpose(beam_pattern, (1, 0, 2))
    corr_t = jnp.transpose(correction, (0, 3, 2, 1))

    order, start = received_order(
        block_tile, block_offset, beam_row, beam_count, beam_dev, blk_beam
    )
    global_slot = (block_tile * TILE_BLK + block_offset).reshape(-1)
    slot_range = beam_row * local_slots + jnp.arange(local_slots, dtype=jnp.int32)
    cover = (global_slot[None, :] == slot_range[:, None]).astype(jnp.float32)
    share = lax.dynamic_slice_in_dim(beam_pattern, chan_part * pixel_share, pixel_share, 2)
    share = share.astype(jnp.float32).reshape(-1, pixel_share)
    weight_sum = jnp.dot(cover, share * share, precision=lax.Precision.HIGHEST)
    inverse = 1.0 / jnp.maximum(weight_sum, floor_value)
    inverse = jnp.swapaxes(inverse.reshape(local_slots, tiles, LANES), 0, 1)
    table = faraday_table(chan_count, chan_dev, DEPTHS)

    spectrum = None
    for first_tile, width in pixel_chunks(tiles):
        sent = send_chunk(
            obs_t, pattern_t, block_tile, corr_t, beam_count, chan_count, first_tile, width
        )
        received = lax.all_to_all(
            sent.reshape((chan_count * beam_count,) + sent.shape[2:]),
            ("chan", "beam"),
            split_axis=0,
            concat_axis=0,
            tiled=True,
        ).reshape(sent.shape)
        spectrum = sky_chunk(
            received,
            inverse,
            table,
            order,
            start,
            first_tile,
            width,
            tiles,
            spectrum,
        )
    return spectrum.reshape(TILE_DEV, TILE_BLK, 2, DEPTHS, pixel_share)


def solution(mesh):
    placed = (P("beam", None, "chan", None, None), P(), P("beam", "chan", None, None), P(), P())
    return jax.shard_map(
        shards,
        mesh=mesh,
        in_specs=placed,
        out_specs=P("beam", None, None, None, "chan"),
        check_vma=False,
    )
```
